128 devices in a mesh: grp: 4 (over z), tile: 32 (over y, x, core).
Axes of the slice: x: 4, y: 4, z: 4, core: 2. Of those that a mesh axis runs over, the one named last changes fastest.
Arguments:
- right_side: float32 [16, 32768], P(None, ('grp', 'tile')), may hold values from -6 to 6
- ridge: float32 [32768], P(('grp', 'tile')), may hold values from 1 to 4
- tiles: float32 [512, 1024, 1024], P(('grp', 'tile')), may hold values from -0.013671875 to 0.013671875
- tile_list: int32 [512, 2], P(('grp', 'tile')), may hold values from 0 to 31, as said below
Outputs:
- solution: float32 [16, 32768], P(None, ('grp', 'tile'))
- residual: float32 [16, 32768], P(None, ('grp', 'tile'))
The draws below stay inside these ranges and needn't reach their ends.
Inputs may be any that keep to these rules, and one draw needn't show every extreme that they name: `tile_list`: each row is a pair (row block, column block) with row block >= column block; no pair appears twice; rows stand in packed row-major order (row block rising, then column block rising).
All inputs are finite; a program needn't handle non-finite values.
Results may differ from the reference program's by a relative error of at most 0.0003.
Values sent between devices are 32-bit elements; how exact they have to be, the bound alone decides.
No kernel may reach another device: no remote copies, remote signals or barrier semaphores. Data moves between devices by JAX's collectives and lax.ppermute only.
A program may use at most 64 MiB of HBM per device.

```python
import math
import jax
import jax.numpy as jnp
from jax import lax

B = 1024
NB = 32
S = 16
ITERS = 2
NP = 32768
NT = 512


def draw_tile_list(key, part):
    total = NB * (NB + 1) // 2
    shuffled = jax.random.permutation(jax.random.fold_in(key, 17), total).astype(jnp.int32)
    dropped = shuffled[:total - NT]
    keep = jnp.ones((total,), jnp.int32).at[dropped].set(0)
    order = jnp.nonzero(keep, size=NT)[0].astype(jnp.int32)
    blocks = jnp.arange(NB, dtype=jnp.int32)
    starts = blocks * (blocks + 1) // 2
    row_block = jnp.sum((starts[None, :] <= order[:, None]).astype(jnp.int32), axis=1) - 1
    row_start = jnp.sum(jnp.where(blocks[None, :] == row_block[:, None], starts[None, :], 0), axis=1)
    col_block = order - row_start
    return jnp.stack([row_block, col_block], axis=1).astype(jnp.int32)


def shard_levels(stream_key, extent, pieces, low, top_value):
    level = 1.0
    for position, parts in pieces:
        draws = jax.random.uniform(jax.random.fold_in(jax.random.fold_in(stream_key, 6), position), (parts,), jnp.float32, low / len(pieces), top_value / len(pieces))
        level = level * jnp.repeat(jnp.exp(draws), extent[position] // parts).reshape((-1,) + (1,) * (len(extent) - 1 - position))
    return level


def bell_draw(rng, extent, spread, most, pieces=(), held_as=jnp.bfloat16):
    result = spread * jax.random.normal(rng, extent, jnp.float32)
    if pieces:
        result = result * shard_levels(rng, extent, pieces, -0.22, 0.18)
    return jnp.clip(result, -most, most).astype(held_as)


def setup_inputs(seed: int = 0) -> dict:
    splits = jax.random.split(jax.random.key(seed), 5)
    right_side = bell_draw(splits[0], (S, NP), 1.0, 6.0, ((1, 128),), jnp.float32)
    ridge = jnp.clip(jnp.exp(math.log(4.0) - 1.3862944 * jax.random.uniform(splits[1], (NP,), jnp.float32) ** shard_levels(splits[1], (NP,), ((0, 128),), -0.2, 0.2)), 1.0, 4.0)
    tiles = bell_draw(splits[2], (NT, B, B), (6 * NB * B) ** -0.5, 0.013671875, ((0, 128),), jnp.float32)
    tile_list = draw_tile_list(jax.random.fold_in(splits[4], 71), 0)
    return dict(right_side=right_side, ridge=ridge, tiles=tiles, tile_list=tile_list)


def gauss_solve(matrix, rhs):
    order = matrix.shape[0]
    for pivot in range(order):
        scale = 1.0 / matrix[pivot, pivot]
        row_new = matrix[pivot] * scale
        rhs_new = rhs[pivot] * scale
        factor = matrix[:, pivot] * (1.0 - (jnp.arange(order) == pivot).astype(matrix.dtype))
        matrix = matrix - factor[:, None] * row_new[None, :]
        rhs = rhs - factor[:, None] * rhs_new[None, :]
        matrix = matrix.at[pivot].set(row_new)
        rhs = rhs.at[pivot].set(rhs_new)
    return rhs


def gram(left, right):
    return lax.dot_general(left, right, (((1,), (1,)), ((), ())), precision=lax.Precision.HIGHEST, preferred_element_type=jnp.float32)


def apply_kernel(tiles, tile_list, field):
    order = tiles.shape[1]
    rowid = lax.broadcasted_iota(jnp.int32, (order, order), 0)
    colid = lax.broadcasted_iota(jnp.int32, (order, order), 1)
    lower = rowid >= colid
    strict = rowid > colid

    def step(total, item):
        tile, pair = item
        block_row = pair[0].astype(jnp.int32)
        block_col = pair[1].astype(jnp.int32)
        differ = block_row != block_col
        direct_tile = jnp.where(jnp.logical_or(lower, differ), tile, jnp.zeros_like(tile))
        mirror_tile = jnp.where(jnp.logical_or(strict, differ), tile, jnp.zeros_like(tile))
        row_start = (block_row * order).astype(jnp.int32)
        col_start = (block_col * order).astype(jnp.int32)
        from_col = lax.dynamic_slice_in_dim(field, col_start, order, 1)
        from_row = lax.dynamic_slice_in_dim(field, row_start, order, 1)
        into_row = lax.dot_general(from_col, direct_tile, (((1,), (1,)), ((), ())), precision=lax.Precision.HIGHEST, preferred_element_type=jnp.float32)
        into_col = jnp.dot(from_row, mirror_tile, precision=lax.Precision.HIGHEST, preferred_element_type=jnp.float32)
        total = lax.dynamic_update_slice_in_dim(total, lax.dynamic_slice_in_dim(total, row_start, order, 1) + into_row, row_start, 1)
        total = lax.dynamic_update_slice_in_dim(total, lax.dynamic_slice_in_dim(total, col_start, order, 1) + into_col, col_start, 1)
        return total, None

    start = jnp.zeros(field.shape, jnp.float32)
    total, _ = lax.scan(step, start, (tiles, tile_list))
    return total


def reference(right_side, ridge, tiles, tile_list):
    solution = jnp.zeros_like(right_side)
    residual = right_side
    direction = right_side
    norm_now = gram(residual, residual)
    for step in range(ITERS):
        image = apply_kernel(tiles, tile_list, direction) + ridge[None, :] * direction
        alpha = gauss_solve(gram(direction, image), norm_now)
        solution = solution + jnp.dot(alpha.T, direction, precision=lax.Precision.HIGHEST)
        residual = residual - jnp.dot(alpha.T, image, precision=lax.Precision.HIGHEST)
        if step + 1 < ITERS:
            norm_next = gram(residual, residual)
            beta = gauss_solve(norm_now, norm_next)
            direction = residual + jnp.dot(beta.T, direction, precision=lax.Precision.HIGHEST)
            norm_now = norm_next
    return solution, residual
```

```python
import functools

import jax
import jax.numpy as jnp
from jax import lax
from jax.experimental import pallas as pl
from jax.experimental.pallas import tpu as pltpu
from jax.sharding import PartitionSpec as P

AXES = ("grp", "tile")
S = 16
B = 1024
NB = 32
D = 128
J = 8
ENDS = 8
R1_ROWS = 12
R2_ROWS = 14
F32 = jnp.float32
BF16 = jnp.bfloat16


def iota(shape, dim):
    return lax.broadcasted_iota(jnp.int32, shape, dim)


def exact(left, right):
    return jnp.dot(left, right, precision=lax.Precision.HIGHEST, preferred_element_type=F32)


def same_column():
    return (iota((D, D), 0) % S == iota((D, D), 1) % S).astype(F32)


def spread_sum(x):
    return exact(x, same_column())


def own_lanes():
    return iota((S, D), 1) // S == iota((S, D), 0) % 8


def flat_rows(g):
    kept = jnp.where(own_lanes(), g, 0.0)
    return jnp.concatenate(
        [jnp.sum(kept[:8], axis=0, keepdims=True), jnp.sum(kept[8:], axis=0, keepdims=True)], axis=0
    )


def from_rows(rows):
    top = jnp.broadcast_to(rows[0:1], (8, D))
    low = jnp.broadcast_to(rows[1:2], (8, D))
    return spread_sum(jnp.where(own_lanes(), jnp.concatenate([top, low], axis=0), 0.0))


def stack8(g):
    return jnp.concatenate([g] * 8, axis=0)


def block_diag(g):
    keep = iota((D, D), 0) // S == iota((D, D), 1) // S
    return jnp.where(keep, stack8(g), 0.0)


def small_mul(left, right):
    return exact(jnp.where(iota((S, D), 1) < S, left, 0.0), stack8(right))


def small_t(g):
    return stack8(g).T[:S]


def owner_gram(left, right):
    both = exact(left.T, right)
    keep = iota((D, D), 0) // S == iota((D, D), 1) // S
    kept = jnp.where(keep, both, 0.0)
    total = kept[0:S]
    for j in range(1, J):
        total = total + kept[j * S : (j + 1) * S]
    return spread_sum(total)


def gauss_solve(matrix, rhs):
    lane = iota((S, D), 1)
    row = iota((S, D), 0)
    work = jnp.where(lane < S, matrix, rhs)
    for pivot in range(S):
        row_new = work[pivot : pivot + 1] * (1.0 / work[pivot : pivot + 1, pivot : pivot + 1])
        factor = jnp.where(row == pivot, 0.0, work[:, pivot : pivot + 1])
        work = jnp.where(row == pivot, row_new, work - factor * row_new)
    return spread_sum(jnp.where((lane >= S) & (lane < 2 * S), work, 0.0))


def pack_kernel(right_ref, ridge_ref, list_ref, out_ref, gram_ref):
    right = right_ref[...]
    ridge = ridge_ref[...]
    rows = [right[:, :D], right[:, D:]]
    rows += [jnp.broadcast_to(ridge[j : j + 1], (S, D)) for j in range(2)]
    rows += [jnp.broadcast_to(list_ref[...], (ENDS, D)), jnp.zeros((D - 4 * S - ENDS, D), F32)]
    out_ref[...] = jnp.concatenate(rows, axis=0).T
    scaled = jnp.concatenate([right[:, :D] * ridge[0:1], right[:, D:] * ridge[1:2]], axis=1)
    nt = (((1,), (1,)), ((), ()))
    tall = jnp.concatenate([right] * 8, axis=0)
    gram_ref[0] = lax.dot_general(
        right, tall, nt, precision=lax.Precision.HIGHEST, preferred_element_type=F32
    )
    gram_ref[1] = lax.dot_general(
        scaled, tall, nt, precision=lax.Precision.HIGHEST, preferred_element_type=F32
    )


def end_matches(ends, k):
    return (ends[:, k : k + 1] == iota((D, NB), 1).astype(F32)).astype(F32)


def send_ends(ends, field, out_ref):
    for k in range(ENDS):
        out_ref[:, k, :] = exact(end_matches(ends, k), field)


def take_ends(ends, got_ref, rows):
    total = jnp.zeros((NB, D), F32)
    for k in range(ENDS):
        part = got_ref[pl.ds(k, D, stride=rows), :]
        total = total + exact(end_matches(ends, k).T, part)
    return total


def take_gram(got_ref, rows, which):
    first = ENDS + 2 * which
    return from_rows(
        jnp.concatenate(
            [
                jnp.sum(got_ref[pl.ds(first + i, D, stride=rows), :], axis=0, keepdims=True)
                for i in range(2)
            ],
            axis=0,
        )
    )


def owner_first_kernel(got_ref, right_ref, ridge_ref, ends_ref, send_ref):
    for target, lanes in ((right_ref, 0), (ridge_ref, 2 * S)):
        target[...] = jnp.concatenate(
            [got_ref[pl.ds(q, NB, stride=4), :][:, lanes : lanes + 2 * S] for q in range(4)], axis=1
        )
    ends = got_ref[...][:, 4 * S : 4 * S + ENDS]
    ends_ref[...] = ends
    send_ends(ends, right_ref[...], send_ref)


def split(x):
    high = x.astype(BF16)
    return high, (x - high.astype(F32)).astype(BF16)


def matvec_kernel(rows, n_grams, list_ref, got_ref, tiles_ref, grams_ref, out_ref, gram_ref):
    t = pl.program_id(0)
    nt = (((1,), (1,)), ((), ()))
    nn = (((1,), (0,)), ((), ()))

    def field(k):
        turned = got_ref[:, k, :].T
        return jnp.concatenate([turned[j * S : (j + 1) * S] for j in range(J)], axis=1)

    def product(vec, high, low, dims):
        vec_high, vec_low = split(vec)
        both = jnp.concatenate([vec_high, vec_low], axis=0)
        main = lax.dot_general(both, high, dims, preferred_element_type=F32)
        rest = lax.dot_general(vec_high, low, dims, preferred_element_type=F32)
        return main[:S] + (main[S:] + rest)

    def put(k, value):
        tall = jnp.concatenate([value[:, j * D : (j + 1) * D] for j in range(J)], axis=0)
        out_ref[pl.ds(k, D, stride=rows), :] = tall.T

    def finish(k, value, vec):
        put(k, value)
        tall = jnp.concatenate([value] * 8, axis=0)
        gram_ref[...] += lax.dot_general(
            vec, tall, nt, precision=lax.Precision.HIGHEST, preferred_element_type=F32
        )

    @pl.when(t == 0)
    def _():
        gram_ref[...] = grams_ref[n_grams - 1]

    def run(step):
        k = 2 * step
        from_row = field(k)
        from_col = field(k + 1)
        diagonal = list_ref[step, 0] == list_ref[step, 1]

        def emit(tile, extra):
            high, low = split(tile)
            finish(k, product(from_col, high, low, nt), from_row)
            into_col = product(from_row, high, low, nn)
            if extra is not None:
                into_col = into_col - from_row * extra
            finish(k + 1, into_col, from_col)

        @pl.when(diagonal)
        def _():
            tile = tiles_ref[0]
            row, col = iota((B, B), 0), iota((B, B), 1)
            middle = jnp.sum(jnp.where(row == col, tile, 0.0), axis=0, keepdims=True)
            emit(jnp.where(row >= col, tile, 0.0), middle)

        @pl.when(jnp.logical_not(diagonal))
        def _():
            emit(tiles_ref[0], None)

    for step in range(4):
        pl.when(t == step)(functools.partial(run, step))

    @pl.when(t == 3)
    def _():
        for which in range(n_grams):
            gram = gram_ref[...] if which == n_grams - 1 else grams_ref[which]
            flat = flat_rows(gram)
            for i in range(2):
                out_ref[pl.ds(ENDS + 2 * which + i, D, stride=rows), :] = jnp.broadcast_to(
                    flat[i : i + 1], (D, D)
                )


def matvec(got, tiles, tile_list, grams, rows):
    n_grams = (rows - ENDS) // 2
    return pl.pallas_call(
        functools.partial(matvec_kernel, rows, n_grams),
        out_shape=jax.ShapeDtypeStruct((D * rows, D), F32),
        grid_spec=pltpu.PrefetchScalarGridSpec(
            num_scalar_prefetch=1,
            grid=(4,),
            in_specs=[
                pl.BlockSpec((D, ENDS, D), lambda t, ref: (0, 0, 0)),
                pl.BlockSpec((1, B, B), lambda t, ref: (t, 0, 0)),
                pl.BlockSpec((n_grams, S, D), lambda t, ref: (0, 0, 0)),
            ],
            out_specs=pl.BlockSpec((D * rows, D), lambda t, ref: (0, 0)),
            scratch_shapes=[pltpu.VMEM((S, D), F32)],
        ),
        compiler_params=pltpu.CompilerParams(
            dimension_semantics=("arbitrary",), vmem_limit_bytes=56 << 20
        ),
        name="matvec",
    )(tile_list, got, tiles, grams)


def owner_middle_kernel(
    got_ref, ends_ref, right_ref, ridge_ref, send_ref, grams_ref, keep_ref, small_ref
):
    ends = ends_ref[...]
    right = right_ref[...]
    ridge = ridge_ref[...]
    image = take_ends(ends, got_ref, R1_ROWS) + ridge * right
    norm = take_gram(got_ref, R1_ROWS, 0)
    curvature = take_gram(got_ref, R1_ROWS, 1)
    alpha = gauss_solve(curvature, norm)
    residual = right - exact(image, block_diag(alpha))
    send_ends(ends, residual, send_ref)
    grams_ref[0] = owner_gram(residual, residual)
    grams_ref[1] = owner_gram(residual, image)
    grams_ref[2] = owner_gram(residual, ridge * residual)
    keep_ref[0] = residual
    keep_ref[1] = image
    small_ref[0] = norm
    small_ref[1] = curvature
    small_ref[2] = alpha


def owner_last_kernel(
    got_ref, ends_ref, right_ref, ridge_ref, keep_ref, small_ref, out_ref, bend_ref
):
    right = right_ref[...]
    residual = keep_ref[0]
    image = keep_ref[1]
    norm, curvature, alpha = small_ref[0], small_ref[1], small_ref[2]
    second = take_ends(ends_ref[...], got_ref, R2_ROWS) + ridge_ref[...] * residual
    norm_next = take_gram(got_ref, R2_ROWS, 0)
    cross = take_gram(got_ref, R2_ROWS, 1)
    bend_ref[...] = take_gram(got_ref, R2_ROWS, 2)
    beta = gauss_solve(norm, norm_next)
    mixed = small_mul(cross, beta)
    bent = bend_ref[...] + mixed + small_t(mixed) + small_mul(small_t(beta), small_mul(curvature, beta))
    last = gauss_solve(bent, norm_next)
    beta_wide = block_diag(beta)
    last_wide = block_diag(last)
    direction = residual + exact(right, beta_wide)
    image_next = second + exact(image, beta_wide)
    solution = exact(right, block_diag(alpha)) + exact(direction, last_wide)
    residual = residual - exact(image_next, last_wide)
    for q in range(4):
        lanes = slice(q * 2 * S, (q + 1) * 2 * S)
        row = jnp.concatenate(
            [solution[:, lanes], residual[:, lanes], jnp.zeros((NB, D - 4 * S), F32)], axis=1
        )
        out_ref[pl.ds(q, NB, stride=4), :] = row


def unpack_kernel(got_ref, solution_ref, residual_ref):
    turned = got_ref[...].T
    for j in range(2):
        solution_ref[:, j * D : (j + 1) * D] = turned[j * S : (j + 1) * S]
        residual_ref[:, j * D : (j + 1) * D] = turned[(2 + j) * S : (3 + j) * S]


def call(kernel, name, shapes, *args, scratch=()):
    return pl.pallas_call(
        kernel,
        out_shape=[jax.ShapeDtypeStruct(shape, F32) for shape in shapes],
        scratch_shapes=[pltpu.VMEM(shape, F32) for shape in scratch],
        compiler_params=pltpu.CompilerParams(vmem_limit_bytes=32 << 20),
        name=name,
    )(*args)


def exchange(x):
    return lax.all_to_all(x, AXES, 0, 0)


def exchange_rows(x, rows):
    return exchange(x.reshape(D, 1, rows * D)).reshape(D * rows, D)


def local(right_side, ridge, tiles, tile_list):
    ends_own = tile_list.reshape(ENDS, 1).astype(F32)
    packed, own_grams = call(
        pack_kernel, "pack", [(D, D), (2, S, D)], right_side, ridge.reshape(2, D), ends_own
    )
    got = exchange_rows(packed, 1)
    right, ridge_wide, ends, send = call(
        owner_first_kernel,
        "owner_first",
        [(NB, D), (NB, D), (D, ENDS), (D, ENDS, D)],
        got,
    )
    got = exchange(send)
    sent = matvec(got, tiles, tile_list, own_grams, R1_ROWS)
    got = exchange_rows(sent, R1_ROWS)
    send, grams, keep, small = call(
        owner_middle_kernel,
        "owner_middle",
        [(D, ENDS, D), (3, S, D), (2, NB, D), (3, S, D)],
        got,
        ends,
        right,
        ridge_wide,
    )
    got = exchange(send)
    sent = matvec(got, tiles, tile_list, grams, R2_ROWS)
    got = exchange_rows(sent, R2_ROWS)
    (packed,) = call(
        owner_last_kernel,
        "owner_last",
        [(D, D)],
        got,
        ends,
        right,
        ridge_wide,
        keep,
        small,
        scratch=[(S, D)],
    )
    got = exchange_rows(packed, 1)
    return tuple(call(unpack_kernel, "unpack", [(S, 2 * D), (S, 2 * D)], got))


def solution(mesh):
    return jax.shard_map(
        local,
        mesh=mesh,
        in_specs=(P(None, AXES), P(AXES), P(AXES, None, None), P(AXES, None)),
        out_specs=(P(None, AXES), P(None, AXES)),
        check_vma=False,
    )
```

```python
import functools

import jax
import jax.numpy as jnp
from jax import lax
from jax.experimental import pallas as pl
from jax.experimental.pallas import tpu as pltpu
from jax.sharding import PartitionSpec as P

CHIPS = ("grp", "ring")
ALL = ("grp", "ring", "core")
S = 16
B = 1024
NB = 32
D = 128
N = 64
J = 8
ENDS = 8
SLOT = 40
RIDGE, NORM, LIST = 32, 34, 36
GRAMS = 32
R1_ROWS = 10
G2_ROWS = 9
F32 = jnp.float32
BF16 = jnp.bfloat16
PIECE = 256
PIECES = B // PIECE
PART = 512
PARTS = B // PART
NT = (((1,), (1,)), ((), ()))
NN = (((1,), (0,)), ((), ()))


def iota(shape, dim):
    return lax.broadcasted_iota(jnp.int32, shape, dim)


def exact(left, right):
    return jnp.dot(left, right, precision=lax.Precision.HIGHEST, preferred_element_type=F32)


def same_column():
    return (iota((D, D), 0) % S == iota((D, D), 1) % S).astype(F32)


def spread_sum(x):
    return exact(x, same_column())


def own_lanes():
    return iota((S, D), 1) // S == iota((S, D), 0) % 8


def flat_rows(g):
    kept = jnp.where(own_lanes(), g, 0.0)
    return jnp.concatenate(
        [jnp.sum(kept[:8], axis=0, keepdims=True), jnp.sum(kept[8:], axis=0, keepdims=True)], axis=0
    )


def from_rows(rows):
    top = jnp.broadcast_to(rows[0:1], (8, D))
    low = jnp.broadcast_to(rows[1:2], (8, D))
    return spread_sum(jnp.where(own_lanes(), jnp.concatenate([top, low], axis=0), 0.0))


def stack8(g):
    return jnp.concatenate([g] * 8, axis=0)


def small_mul(left, right):
    return exact(jnp.where(iota((S, D), 1) < S, left, 0.0), stack8(right))


def small_t(g):
    return stack8(g).T[:S]


def gram(left, right):
    return lax.dot_general(
        left, right, NT, precision=lax.Precision.HIGHEST, preferred_element_type=F32
    )


def widen(g):
    return jnp.concatenate([g] * 8, axis=1)


def mixed(coeffs, rows):
    return exact(small_t(coeffs)[:, :S], rows)


def gauss_solve(matrix, rhs):
    lane = iota((S, D), 1)
    row = iota((S, D), 0)
    work = jnp.where(lane < S, matrix, rhs)
    for pivot in range(S):
        row_new = work[pivot : pivot + 1] * (1.0 / work[pivot : pivot + 1, pivot : pivot + 1])
        factor = jnp.where(row == pivot, 0.0, work[:, pivot : pivot + 1])
        work = jnp.where(row == pivot, row_new, work - factor * row_new)
    return spread_sum(jnp.where((lane >= S) & (lane < 2 * S), work, 0.0))


def gather_pack_kernel(right_ref, ridge_ref, list_ref, out_ref):
    right = right_ref[...]
    rows = [right[:, :D], right[:, D:], ridge_ref[...], flat_rows(widen(gram(right, right)))]
    slot = iota((1, D), 1)
    ends = jnp.zeros((1, D), F32)
    for k in range(ENDS):
        ends = jnp.where(slot == k, list_ref[k // 2, k % 2].astype(F32), ends)
    rows += [ends, jnp.zeros((SLOT - LIST - 1, D), F32)]
    packed = jnp.concatenate(rows, axis=0)
    for chip in range(N):
        out_ref[chip] = packed


def split(x):
    high = x.astype(BF16)
    return high, (x - high.astype(F32)).astype(BF16)


def stage_kernel(list_ref, tiles_ref, high_ref, low_ref, held, high, low, in_sems, out_sems):
    def fetch(i):
        rows = pl.ds(i % PIECES * PIECE, PIECE)
        return pltpu.make_async_copy(tiles_ref.at[i // PIECES, rows], held.at[i], in_sems.at[i])

    def flush(i):
        rows = pl.ds(i % PIECES * PIECE, PIECE)
        return [
            pltpu.make_async_copy(here.at[i], there.at[i // PIECES, rows], out_sems.at[which, i])
            for which, (here, there) in enumerate(((high, high_ref), (low, low_ref)))
        ]

    for i in range(4 * PIECES):
        fetch(i).start()
    for i in range(4 * PIECES):
        fetch(i).wait()
        tile, first = i // PIECES, i % PIECES * PIECE
        high[i], low[i] = split(held[i])

        @pl.when(list_ref[tile, 0] == list_ref[tile, 1])
        def _():
            row, col = iota((PIECE, B), 0) + first, iota((PIECE, B), 1)
            kept = jnp.where(row > col, held[i], jnp.where(row == col, 0.5 * held[i], 0.0))
            high[i], low[i] = split(kept)

        for copy in flush(i):
            copy.start()
    for i in range(4 * PIECES):
        for copy in flush(i):
            copy.wait()


def stage(tiles, tile_list):
    anywhere = pl.BlockSpec(memory_space=pltpu.HBM)
    return pl.pallas_call(
        stage_kernel,
        out_shape=[pltpu.HBM((4, B, B), BF16)] * 2,
        in_specs=[pl.BlockSpec(memory_space=pltpu.SMEM), anywhere],
        out_specs=[anywhere] * 2,
        scratch_shapes=[
            pltpu.VMEM((4 * PIECES, PIECE, B), F32),
            pltpu.VMEM((4 * PIECES, PIECE, B), BF16),
            pltpu.VMEM((4 * PIECES, PIECE, B), BF16),
            pltpu.SemaphoreType.DMA((4 * PIECES,)),
            pltpu.SemaphoreType.DMA((2, 4 * PIECES)),
        ],
        compiler_params=pltpu.CompilerParams(vmem_limit_bytes=40 << 20),
        name="stage",
    )(tile_list, tiles)


def by_core(mine, other):
    first = lax.axis_index("core") == 0
    return jnp.where(first, mine, other), jnp.where(first, other, mine)


def block_of(mine_ref, other_ref, block):
    field, ridge = [], []
    for half in range(2):
        chip = 2 * block + half
        for piece in by_core(mine_ref[chip], other_ref[chip]):
            field += [piece[:S], piece[S : 2 * S]]
            ridge += [piece[RIDGE : RIDGE + 1], piece[RIDGE + 1 : RIDGE + 2]]
    return jnp.concatenate(field, axis=1), jnp.concatenate(ridge, axis=1)


def fetch_parts(high_hbm, low_hbm, high_ref, low_ref, sems):
    def fetch(i):
        part = (i // PARTS, pl.ds(i % PARTS * PART, PART))
        return [
            pltpu.make_async_copy(there.at[part], here.at[part], sems.at[which, i])
            for which, (there, here) in enumerate(((high_hbm, high_ref), (low_hbm, low_ref)))
        ]

    for i in range(4 * PARTS):
        for copy in fetch(i):
            copy.start()
    return fetch


def multiply(fetch, high_ref, low_ref, field, put):
    def product(vec, tile, part, dims):
        vec_high, vec_low = split(vec)
        both = jnp.concatenate([vec_high, vec_low], axis=0)
        main = lax.dot_general(both, high_ref[tile, part], dims, preferred_element_type=F32)
        rest = lax.dot_general(vec_high, low_ref[tile, part], dims, preferred_element_type=F32)
        return main[:S] + (main[S:] + rest)

    half = jnp.zeros((S, S), F32)
    for tile in range(4):
        from_row, from_col = field(2 * tile), field(2 * tile + 1)
        into_row, into_col = [], []
        for part in range(PARTS):
            for copy in fetch(tile * PARTS + part):
                copy.wait()
            at = slice(part * PART, (part + 1) * PART)
            into_row.append(product(from_col, tile, at, NT))
            into_col.append(product(from_row[:, at], tile, at, NN))
        into_row = jnp.concatenate(into_row, axis=1)
        put(2 * tile, into_row)
        put(2 * tile + 1, sum(into_col[1:], into_col[0]))
        half = half + gram(from_row, into_row)
    return half + half.T


def first_kernel(
    list_ref, mine_ref, other_ref, right_ref, ridge_ref, high_hbm, low_hbm, out_ref,
    high_ref, low_ref, gram_ref, sems,
):
    fetch = fetch_parts(high_hbm, low_hbm, high_ref, low_ref, sems)

    def field(k):
        return block_of(mine_ref, other_ref, list_ref[k // 2, k % 2])[0]

    def put(k, value):
        tall = jnp.concatenate([value[:, j * D : (j + 1) * D] for j in range(J)], axis=0)
        out_ref[pl.ds(k, D, stride=R1_ROWS), :] = tall.T

    right = right_ref[...]
    ridge = jnp.concatenate([ridge_ref[0:1], ridge_ref[1:2]], axis=1)
    gram_ref[...] = gram(right, ridge * right)
    curvature = multiply(fetch, high_ref, low_ref, field, put)
    flat = flat_rows(widen(gram_ref[...] + curvature))
    for i in range(2):
        out_ref[pl.ds(ENDS + i, D, stride=R1_ROWS), :] = jnp.broadcast_to(flat[i : i + 1], (D, D))


def end_matches(ends, k):
    return (ends[:, k : k + 1] == iota((D, NB), 1).astype(F32)).astype(F32)


def owner_kernel(got_ref, mine_ref, other_ref, out_ref, ends_ref):
    even, odd = by_core(mine_ref[:, LIST, :], other_ref[:, LIST, :])
    ends_ref[pl.ds(0, N, stride=2), :] = even
    ends_ref[pl.ds(1, N, stride=2), :] = odd
    ends = ends_ref[...]
    total = jnp.zeros((NB, D), F32)
    for k in range(ENDS):
        part = got_ref[pl.ds(k, D, stride=R1_ROWS), :]
        total = total + exact(end_matches(ends, k).T, part)
    for k in range(ENDS):
        out_ref[pl.ds(k, D, stride=G2_ROWS), :] = exact(end_matches(ends, k), total)
    for q in range(4):
        own = [total[:, 2 * S * q : 2 * S * (q + 1)], jnp.zeros((NB, D - 2 * S), F32)]
        out_ref[pl.ds(G2_ROWS * q + ENDS, NB, stride=4 * G2_ROWS), :] = jnp.concatenate(own, axis=1)


def alpha_kernel(got_ref, mine_ref, other_ref, out_ref):
    curvature, norm = [], []
    for i in range(2):
        part = got_ref[pl.ds(ENDS + i, D, stride=R1_ROWS), :]
        curvature.append(jnp.sum(part, axis=0, keepdims=True))
        part = mine_ref[:, NORM + i, :] + other_ref[:, NORM + i, :]
        norm.append(jnp.sum(part, axis=0, keepdims=True))
    out_ref[0] = from_rows(jnp.concatenate(norm, axis=0))
    out_ref[1] = from_rows(jnp.concatenate(curvature, axis=0))
    out_ref[2] = gauss_solve(out_ref[1], out_ref[0])


def second_kernel(
    list_ref, mine_ref, other_ref, right_ref, ridge_ref, got_ref, small_ref, high_hbm, low_hbm,
    out_ref, keep_ref, high_ref, low_ref, gram_ref, sems,
):
    fetch = fetch_parts(high_hbm, low_hbm, high_ref, low_ref, sems)
    alpha_t = small_t(small_ref[2])[:, :S]

    def field(k):
        right, ridge = block_of(mine_ref, other_ref, list_ref[k // 2, k % 2])
        turned = got_ref[pl.ds(k, D, stride=G2_ROWS), :].T
        image = jnp.concatenate([turned[j * S : (j + 1) * S] for j in range(J)], axis=1)
        return right - exact(alpha_t, image + ridge * right)

    core = lax.axis_index("core")
    out_ref[...] = jnp.zeros(out_ref.shape, F32)

    def put(k, value):
        block = list_ref[k // 2, k % 2]
        for q in range(4):
            chip, side = 2 * block + q // 2, (q % 2 + core) % 2
            for j in range(2):
                rows = slice(j * S, (j + 1) * S)
                lanes = slice((2 * q + j) * D, (2 * q + j + 1) * D)
                out_ref[side, chip, rows] = out_ref[side, chip, rows] + value[:, lanes]

    right = right_ref[...]
    ridge = jnp.concatenate([ridge_ref[0:1], ridge_ref[1:2]], axis=1)
    turned = got_ref[pl.ds(ENDS, D, stride=G2_ROWS), :].T
    image = jnp.concatenate([turned[:S], turned[S : 2 * S]], axis=1) + ridge * right
    residual = right - exact(alpha_t, image)
    keep_ref[0] = residual
    keep_ref[1] = image
    gram_ref[0] = gram(residual, residual)
    gram_ref[1] = gram(residual, image)
    gram_ref[2] = gram(residual, ridge * residual)
    gram_ref[2] += multiply(fetch, high_ref, low_ref, field, put)
    flat = jnp.concatenate(
        [flat_rows(widen(gram_ref[i])) for i in range(3)] + [jnp.zeros((2, D), F32)], axis=0
    )
    for side in range(2):
        for chip in range(N):
            out_ref[side, chip, GRAMS:] = flat


def last_kernel(
    got_ref, right_ref, ridge_ref, keep_ref, small_ref, solution_ref, residual_ref, gram_ref
):
    total = got_ref[0]
    for chip in range(1, N):
        total = total + got_ref[chip]
    right = right_ref[...]
    residual, image = keep_ref[0], keep_ref[1]
    ridge = jnp.concatenate([ridge_ref[0:1], ridge_ref[1:2]], axis=1)
    second = jnp.concatenate([total[:S], total[S : 2 * S]], axis=1) + ridge * residual
    for i in range(3):
        gram_ref[i] = from_rows(total[GRAMS + 2 * i : GRAMS + 2 * i + 2])
    beta = gauss_solve(small_ref[0], gram_ref[0])
    gram_ref[3] = small_mul(gram_ref[1], beta)
    gram_ref[4] = small_mul(small_t(beta), small_mul(small_ref[1], beta))
    bent = gram_ref[2] + gram_ref[3] + small_t(gram_ref[3]) + gram_ref[4]
    last = gauss_solve(bent, gram_ref[0])
    direction = residual + mixed(beta, right)
    image_next = second + mixed(beta, image)
    solution_ref[...] = mixed(small_ref[2], right) + mixed(last, direction)
    residual_ref[...] = residual - mixed(last, image_next)


HERE = pl.BlockSpec(memory_space=pltpu.VMEM)
SCALARS = pl.BlockSpec(memory_space=pltpu.SMEM)
THERE = pl.BlockSpec(memory_space=pltpu.HBM)
STAGED = [
    pltpu.VMEM((4, B, B), BF16),
    pltpu.VMEM((4, B, B), BF16),
]


def call(kernel, name, shapes, specs, args, scratch=(), limit=32):
    return pl.pallas_call(
        kernel,
        out_shape=[jax.ShapeDtypeStruct(shape, F32) for shape in shapes],
        in_specs=specs,
        out_specs=[HERE] * len(shapes),
        scratch_shapes=scratch,
        compiler_params=pltpu.CompilerParams(vmem_limit_bytes=limit << 20),
        name=name,
    )(*args)


def exchange_rows(x, rows):
    return lax.all_to_all(x.reshape(D, 1, rows * D), ALL, 0, 0).reshape(D * rows, D)


def swap(x):
    return lax.ppermute(x, "core", [(0, 1), (1, 0)])


def local(right, ridge, tiles, tile_list):
    ridge = ridge.reshape(2, D)
    (packed,) = call(
        gather_pack_kernel, "pack", [(N, SLOT, D)], [HERE, HERE, SCALARS], (right, ridge, tile_list)
    )
    later_list, packed = lax.optimization_barrier((tile_list, packed))
    staged = stage(tiles, later_list)
    mine = lax.all_to_all(packed, CHIPS, 0, 0)
    mine, *staged = lax.optimization_barrier((mine, *staged))
    other = swap(mine)
    sems = pltpu.SemaphoreType.DMA((2, 4 * PARTS))
    (sent,) = call(
        first_kernel,
        "first",
        [(D * R1_ROWS, D)],
        [SCALARS] + [HERE] * 4 + [THERE] * 2,
        (tile_list, mine, other, right, ridge, *staged),
        [*STAGED, pltpu.VMEM((S, S), F32), sems],
        48,
    )
    got = exchange_rows(sent, R1_ROWS)
    (sent,) = call(
        owner_kernel,
        "owner",
        [(D * G2_ROWS, D)],
        [HERE] * 3,
        (got, mine, other),
        [pltpu.VMEM((D, D), F32)],
    )
    (small,) = call(alpha_kernel, "alpha", [(3, S, D)], [HERE] * 3, (got, mine, other))
    got = exchange_rows(sent, G2_ROWS)
    sent, keep = call(
        second_kernel,
        "second",
        [(2, N, SLOT, D), (2, S, 2 * D)],
        [SCALARS] + [HERE] * 6 + [THERE] * 2,
        (tile_list, mine, other, right, ridge, got, small, *staged),
        [*STAGED, pltpu.VMEM((3, S, S), F32), sems],
        48,
    )
    got = lax.all_to_all(sent[0] + swap(sent[1]), CHIPS, 0, 0)
    return tuple(
        call(
            last_kernel,
            "last",
            [(S, 2 * D)] * 2,
            [HERE] * 5,
            (got, right, ridge, keep, small),
            [pltpu.VMEM((5, S, D), F32)],
        )
    )


def solution(mesh):
    mesh = jax.sharding.Mesh(mesh.devices.reshape(4, 16, 2), ALL)
    return jax.shard_map(
        local,
        mesh=mesh,
        in_specs=(P(None, ALL), P(ALL), P(ALL, None, None), P(ALL, None)),
        out_specs=(P(None, ALL), P(None, ALL)),
        check_vma=False,
    )
```

```python
import functools

import jax
import jax.numpy as jnp
from jax import lax
from jax.experimental import pallas as pl
from jax.experimental.pallas import tpu as pltpu
from jax.sharding import PartitionSpec as P

CHIPS = ("grp", "ring")
ALL = ("grp", "ring", "core")
S = 16
B = 1024
NB = 32
D = 128
N = 64
J = 8
ENDS = 8
GATHER = 32
OWN = 10
SLOT = 40
GRAMS = 32
R1_ROWS = 11
G2_ROWS = 9
F32 = jnp.float32
BF16 = jnp.bfloat16
PIECE = 256
PIECES = B // PIECE
PARTS = [(0, 0, 256), (0, 256, 256), (0, 512, 512)]
PARTS += [(tile, first, 512) for tile in range(1, 4) for first in (0, 512)]
NT = (((1,), (1,)), ((), ()))
NN = (((1,), (0,)), ((), ()))


def iota(shape, dim):
    return lax.broadcasted_iota(jnp.int32, shape, dim)


def exact(left, right):
    return jnp.dot(left, right, precision=lax.Precision.HIGHEST, preferred_element_type=F32)


def same_column():
    return (iota((D, D), 0) % S == iota((D, D), 1) % S).astype(F32)


def spread_sum(x):
    return exact(x, same_column())


def own_lanes():
    return iota((S, D), 1) // S == iota((S, D), 0) % 8


def flat_rows(g):
    kept = jnp.where(own_lanes(), g, 0.0)
    return jnp.concatenate(
        [jnp.sum(kept[:8], axis=0, keepdims=True), jnp.sum(kept[8:], axis=0, keepdims=True)], axis=0
    )


def from_rows(rows):
    top = jnp.broadcast_to(rows[0:1], (8, D))
    low = jnp.broadcast_to(rows[1:2], (8, D))
    return spread_sum(jnp.where(own_lanes(), jnp.concatenate([top, low], axis=0), 0.0))


def stack8(g):
    return jnp.concatenate([g] * 8, axis=0)


def small_mul(left, right):
    return exact(jnp.where(iota((S, D), 1) < S, left, 0.0), stack8(right))


def small_t(g):
    return stack8(g).T[:S]


def gram(left, right):
    return lax.dot_general(
        left, right, NT, precision=lax.Precision.HIGHEST, preferred_element_type=F32
    )


def widen(g):
    return jnp.concatenate([g] * 8, axis=1)


def mixed(coeffs, rows):
    return exact(small_t(coeffs)[:, :S], rows)


def gauss_solve(matrix, rhs):
    lane = iota((S, D), 1)
    row = iota((S, D), 0)
    work = jnp.where(lane < S, matrix, rhs)
    for pivot in range(S):
        row_new = work[pivot : pivot + 1] * (1.0 / work[pivot : pivot + 1, pivot : pivot + 1])
        factor = jnp.where(row == pivot, 0.0, work[:, pivot : pivot + 1])
        work = jnp.where(row == pivot, row_new, work - factor * row_new)
    return spread_sum(jnp.where((lane >= S) & (lane < 2 * S), work, 0.0))


def gather_pack_kernel(right_ref, out_ref):
    right = right_ref[...]
    packed = jnp.concatenate([right[:, :D], right[:, D:]], axis=0)
    for chip in range(N):
        out_ref[chip] = packed


def split(x):
    high = x.astype(BF16)
    return high, (x - high.astype(F32)).astype(BF16)


def stage_kernel(list_ref, tiles_ref, high_ref, low_ref, held, high, low, in_sems, out_sems):
    def fetch(i):
        rows = pl.ds(i % PIECES * PIECE, PIECE)
        return pltpu.make_async_copy(tiles_ref.at[i // PIECES, rows], held.at[i], in_sems.at[i])

    def flush(i):
        rows = pl.ds(i % PIECES * PIECE, PIECE)
        return [
            pltpu.make_async_copy(here.at[i], there.at[i // PIECES, rows], out_sems.at[which, i])
            for which, (here, there) in enumerate(((high, high_ref), (low, low_ref)))
        ]

    for i in range(4 * PIECES):
        fetch(i).start()
    for i in range(4 * PIECES):
        fetch(i).wait()
        tile, first = i // PIECES, i % PIECES * PIECE
        high[i], low[i] = split(held[i])

        @pl.when(list_ref[0, tile] == list_ref[1, tile])
        def _():
            row, col = iota((PIECE, B), 0) + first, iota((PIECE, B), 1)
            kept = jnp.where(row > col, held[i], jnp.where(row == col, 0.5 * held[i], 0.0))
            high[i], low[i] = split(kept)

        for copy in flush(i):
            copy.start()
    for i in range(4 * PIECES):
        for copy in flush(i):
            copy.wait()


def stage(tiles, tile_list):
    anywhere = pl.BlockSpec(memory_space=pltpu.HBM)
    return pl.pallas_call(
        stage_kernel,
        out_shape=[pltpu.HBM((4, B, B), BF16)] * 2,
        in_specs=[pl.BlockSpec(memory_space=pltpu.SMEM), anywhere],
        out_specs=[anywhere] * 2,
        scratch_shapes=[
            pltpu.VMEM((4 * PIECES, PIECE, B), F32),
            pltpu.VMEM((4 * PIECES, PIECE, B), BF16),
            pltpu.VMEM((4 * PIECES, PIECE, B), BF16),
            pltpu.SemaphoreType.DMA((4 * PIECES,)),
            pltpu.SemaphoreType.DMA((2, 4 * PIECES)),
        ],
        compiler_params=pltpu.CompilerParams(vmem_limit_bytes=40 << 20),
        name="stage",
    )(tile_list, tiles)


def by_core(mine, other):
    first = lax.axis_index("core") == 0
    return jnp.where(first, mine, other), jnp.where(first, other, mine)


def block_of(mine_ref, other_ref, block):
    field = []
    for half in range(2):
        chip = 2 * block + half
        for piece in by_core(mine_ref[chip], other_ref[chip]):
            field += [piece[:S], piece[S:]]
    return jnp.concatenate(field, axis=1)


def fetch_parts(high_hbm, low_hbm, high_ref, low_ref, sems):
    def fetch(i):
        tile, first, rows = PARTS[i]
        part = (tile, pl.ds(first, rows))
        return [
            pltpu.make_async_copy(there.at[part], here.at[part], sems.at[which, i])
            for which, (there, here) in enumerate(((high_hbm, high_ref), (low_hbm, low_ref)))
        ]

    for i in range(len(PARTS)):
        for copy in fetch(i):
            copy.start()
    return fetch


def multiply(fetch, high_ref, low_ref, field, put):
    def product(vec, tile, part, dims):
        vec_high, vec_low = split(vec)
        both = jnp.concatenate([vec_high, vec_low], axis=0)
        main = lax.dot_general(both, high_ref[tile, part], dims, preferred_element_type=F32)
        rest = lax.dot_general(vec_high, low_ref[tile, part], dims, preferred_element_type=F32)
        return main[:S] + (main[S:] + rest)

    half = jnp.zeros((S, S), F32)
    for tile in range(4):
        from_row, from_col = field(2 * tile), field(2 * tile + 1)
        into_row, into_col = [], []
        for i, (owner, first, rows) in enumerate(PARTS):
            if owner != tile:
                continue
            for copy in fetch(i):
                copy.wait()
            at = slice(first, first + rows)
            into_row.append(product(from_col, tile, at, NT))
            into_col.append(product(from_row[:, at], tile, at, NN))
        into_row = jnp.concatenate(into_row, axis=1)
        put(2 * tile, into_row)
        put(2 * tile + 1, sum(into_col[1:], into_col[0]))
        half = half + gram(from_row, into_row)
    return half + half.T


def first_kernel(
    list_ref, mine_ref, other_ref, right_ref, ridge_ref, high_hbm, low_hbm, out_ref,
    high_ref, low_ref, gram_ref, sems,
):
    fetch = fetch_parts(high_hbm, low_hbm, high_ref, low_ref, sems)

    def field(k):
        return block_of(mine_ref, other_ref, list_ref[k % 2, k // 2])

    def put(k, value):
        tall = jnp.concatenate([value[:, j * D : (j + 1) * D] for j in range(J)], axis=0)
        out_ref[pl.ds(k, D, stride=R1_ROWS), :] = tall.T

    right = right_ref[...]
    scaled = jnp.concatenate([ridge_ref[0:1], ridge_ref[1:2]], axis=1) * right
    gram_ref[...] = gram(right, scaled)
    slot = iota((ENDS, D), 0)
    ends = jnp.zeros((ENDS, D), F32)
    for k in range(ENDS):
        ends = jnp.where(slot == k, list_ref[k % 2, k // 2].astype(F32), ends)
    own = [scaled[:, :D], scaled[:, D:], ends, jnp.zeros((D - 2 * S - ENDS, D), F32)]
    out_ref[pl.ds(OWN, D, stride=R1_ROWS), :] = jnp.concatenate(own, axis=0).T
    curvature = multiply(fetch, high_ref, low_ref, field, put)
    flat = flat_rows(widen(gram_ref[...] + curvature))
    for i in range(2):
        out_ref[pl.ds(ENDS + i, D, stride=R1_ROWS), :] = jnp.broadcast_to(flat[i : i + 1], (D, D))


def end_matches(ends, k):
    return ends[:, k : k + 1] == iota((D, NB), 1).astype(F32)


def select(matches, values):
    high, rest = split(values)
    low = (values - high.astype(F32) - rest.astype(F32)).astype(BF16)
    parts = jnp.dot(
        matches.astype(F32).astype(BF16),
        jnp.concatenate([high, rest, low], axis=1),
        preferred_element_type=F32,
    )
    return parts[:, :D] + parts[:, D : 2 * D] + parts[:, 2 * D :]


def owner_kernel(got_ref, out_ref):
    own = [got_ref[pl.ds(R1_ROWS * q + OWN, NB, stride=4 * R1_ROWS), :] for q in range(4)]
    total = jnp.concatenate([part[:, : 2 * S] for part in own], axis=1)
    ends = got_ref[pl.ds(OWN, D, stride=R1_ROWS), :][:, 2 * S : 2 * S + ENDS]
    for k in range(ENDS):
        part = got_ref[pl.ds(k, D, stride=R1_ROWS), :]
        total = total + select(end_matches(ends, k).astype(F32).T, part)
    for k in range(ENDS):
        out_ref[pl.ds(k, D, stride=G2_ROWS), :] = select(end_matches(ends, k), total)
    for q in range(4):
        own = [total[:, 2 * S * q : 2 * S * (q + 1)], jnp.zeros((NB, D - 2 * S), F32)]
        out_ref[pl.ds(G2_ROWS * q + ENDS, NB, stride=4 * G2_ROWS), :] = jnp.concatenate(own, axis=1)


def alpha_kernel(got_ref, mine_ref, other_ref, out_ref, norm_ref):
    norm_ref[...] = jnp.zeros((S, S), F32)
    for ref in (mine_ref, other_ref):

        @pl.loop(0, N, step=4)
        def _(chip):
            pieces = [ref[chip + i] for i in range(4)]
            wide = jnp.concatenate([half for p in pieces for half in (p[:S], p[S:])], axis=1)
            norm_ref[...] += gram(wide, wide)

    curvature = []
    for i in range(2):
        part = got_ref[pl.ds(ENDS + i, D, stride=R1_ROWS), :]
        curvature.append(jnp.sum(part, axis=0, keepdims=True))
    out_ref[0] = widen(norm_ref[...])
    out_ref[1] = from_rows(jnp.concatenate(curvature, axis=0))
    out_ref[2] = gauss_solve(out_ref[1], out_ref[0])


def second_kernel(
    list_ref, mine_ref, other_ref, right_ref, ridge_ref, got_ref, small_ref, high_hbm, low_hbm,
    out_ref, keep_ref, high_ref, low_ref, gram_ref, sems,
):
    fetch = fetch_parts(high_hbm, low_hbm, high_ref, low_ref, sems)
    alpha_t = small_t(small_ref[2])[:, :S]

    def field(k):
        turned = got_ref[pl.ds(k, D, stride=G2_ROWS), :].T
        image = jnp.concatenate([turned[j * S : (j + 1) * S] for j in range(J)], axis=1)
        return block_of(mine_ref, other_ref, list_ref[k % 2, k // 2]) - exact(alpha_t, image)

    core = lax.axis_index("core")
    out_ref[...] = jnp.zeros(out_ref.shape, F32)

    def put(k, value):
        block = list_ref[k % 2, k // 2]
        for q in range(4):
            chip, side = 2 * block + q // 2, (q % 2 + core) % 2
            for j in range(2):
                rows = slice(j * S, (j + 1) * S)
                lanes = slice((2 * q + j) * D, (2 * q + j + 1) * D)
                out_ref[side, chip, rows] = out_ref[side, chip, rows] + value[:, lanes]

    right = right_ref[...]
    ridge = jnp.concatenate([ridge_ref[0:1], ridge_ref[1:2]], axis=1)
    turned = got_ref[pl.ds(ENDS, D, stride=G2_ROWS), :].T
    image = jnp.concatenate([turned[:S], turned[S : 2 * S]], axis=1)
    residual = right - exact(alpha_t, image)
    keep_ref[0] = residual
    keep_ref[1] = image
    gram_ref[0] = gram(residual, residual)
    gram_ref[1] = gram(residual, image)
    gram_ref[2] = gram(residual, ridge * residual)
    gram_ref[2] += multiply(fetch, high_ref, low_ref, field, put)
    flat = jnp.concatenate(
        [flat_rows(widen(gram_ref[i])) for i in range(3)] + [jnp.zeros((2, D), F32)], axis=0
    )
    for side in range(2):
        for chip in range(N):
            out_ref[side, chip, GRAMS:] = flat


def last_kernel(
    got_ref, right_ref, ridge_ref, keep_ref, small_ref, solution_ref, residual_ref, gram_ref
):
    total = got_ref[0]
    for chip in range(1, N):
        total = total + got_ref[chip]
    right = right_ref[...]
    residual, image = keep_ref[0], keep_ref[1]
    ridge = jnp.concatenate([ridge_ref[0:1], ridge_ref[1:2]], axis=1)
    second = jnp.concatenate([total[:S], total[S : 2 * S]], axis=1) + ridge * residual
    for i in range(3):
        gram_ref[i] = from_rows(total[GRAMS + 2 * i : GRAMS + 2 * i + 2])
    beta = gauss_solve(small_ref[0], gram_ref[0])
    gram_ref[3] = small_mul(gram_ref[1], beta)
    gram_ref[4] = small_mul(small_t(beta), small_mul(small_ref[1], beta))
    bent = gram_ref[2] + gram_ref[3] + small_t(gram_ref[3]) + gram_ref[4]
    last = gauss_solve(bent, gram_ref[0])
    direction = residual + mixed(beta, right)
    image_next = second + mixed(beta, image)
    solution_ref[...] = mixed(small_ref[2], right) + mixed(last, direction)
    residual_ref[...] = residual - mixed(last, image_next)


HERE = pl.BlockSpec(memory_space=pltpu.VMEM)
SCALARS = pl.BlockSpec(memory_space=pltpu.SMEM)
THERE = pl.BlockSpec(memory_space=pltpu.HBM)
STAGED = [
    pltpu.VMEM((4, B, B), BF16),
    pltpu.VMEM((4, B, B), BF16),
]


def call(kernel, name, shapes, specs, args, scratch=(), limit=32):
    return pl.pallas_call(
        kernel,
        out_shape=[jax.ShapeDtypeStruct(shape, F32) for shape in shapes],
        in_specs=specs,
        out_specs=[HERE] * len(shapes),
        scratch_shapes=scratch,
        compiler_params=pltpu.CompilerParams(vmem_limit_bytes=limit << 20),
        name=name,
    )(*args)


def exchange_rows(x, rows):
    return lax.all_to_all(x.reshape(D, 1, rows * D), ALL, 0, 0).reshape(D * rows, D)


def swap(x):
    return lax.ppermute(x, "core", [(0, 1), (1, 0)])


def local(right, ridge, tiles, tile_list):
    ridge = ridge.reshape(2, D)
    tile_list = tile_list.T
    (packed,) = call(gather_pack_kernel, "pack", [(N, GATHER, D)], [HERE], (right,))
    later_list, packed = lax.optimization_barrier((tile_list, packed))
    staged = stage(tiles, later_list)
    mine = lax.all_to_all(packed, CHIPS, 0, 0)
    mine, *staged = lax.optimization_barrier((mine, *staged))
    other = swap(mine)
    sems = pltpu.SemaphoreType.DMA((2, len(PARTS)))
    (sent,) = call(
        first_kernel,
        "first",
        [(D * R1_ROWS, D)],
        [SCALARS] + [HERE] * 4 + [THERE] * 2,
        (tile_list, mine, other, right, ridge, *staged),
        [*STAGED, pltpu.VMEM((S, S), F32), sems],
        48,
    )
    got = exchange_rows(sent, R1_ROWS)
    (sent,) = call(
        owner_kernel,
        "owner",
        [(D * G2_ROWS, D)],
        [HERE],
        (got,),
    )
    (small,) = call(
        alpha_kernel,
        "alpha",
        [(3, S, D)],
        [HERE] * 3,
        (got, mine, other),
        [pltpu.VMEM((S, S), F32)],
    )
    got = exchange_rows(sent, G2_ROWS)
    sent, keep = call(
        second_kernel,
        "second",
        [(2, N, SLOT, D), (2, S, 2 * D)],
        [SCALARS] + [HERE] * 6 + [THERE] * 2,
        (tile_list, mine, other, right, ridge, got, small, *staged),
        [*STAGED, pltpu.VMEM((3, S, S), F32), sems],
        48,
    )
    got = lax.all_to_all(sent[0] + swap(sent[1]), CHIPS, 0, 0)
    return tuple(
        call(
            last_kernel,
            "last",
            [(S, 2 * D)] * 2,
            [HERE] * 5,
            (got, right, ridge, keep, small),
            [pltpu.VMEM((5, S, D), F32)],
        )
    )


def solution(mesh):
    mesh = jax.sharding.Mesh(mesh.devices.reshape(4, 16, 2), ALL)
    return jax.shard_map(
        local,
        mesh=mesh,
        in_specs=(P(None, ALL), P(ALL), P(ALL, None, None), P(ALL, None)),
        out_specs=(P(None, ALL), P(None, ALL)),
        check_vma=False,
    )
```

```python
import functools

import jax
import jax.numpy as jnp
from jax import lax
from jax.experimental import pallas as pl
from jax.experimental.pallas import tpu as pltpu
from jax.sharding import PartitionSpec as P

CHIPS = ("grp", "ring")
ALL = ("grp", "ring", "core")
S = 16
B = 1024
NB = 32
D = 128
N = 64
J = 8
ENDS = 8
REST = 64
OWN = 9
SLOT = 40
GRAMS = 32
R1_ROWS = 10
G2_ROWS = 9
F32 = jnp.float32
BF16 = jnp.bfloat16
PIECE = 256
PIECES = B // PIECE
PARTS = [(0, 0, 256), (0, 256, 256), (0, 512, 512)]
PARTS += [(tile, first, 512) for tile in range(1, 4) for first in (0, 512)]
NT = (((1,), (1,)), ((), ()))
NN = (((1,), (0,)), ((), ()))


def iota(shape, dim):
    return lax.broadcasted_iota(jnp.int32, shape, dim)


def exact(left, right):
    return jnp.dot(left, right, precision=lax.Precision.HIGHEST, preferred_element_type=F32)


def same_column():
    return (iota((D, D), 0) % S == iota((D, D), 1) % S).astype(F32)


def spread_sum(x):
    return exact(x, same_column())


def own_lanes():
    return iota((S, D), 1) // S == iota((S, D), 0) % 8


def flat_rows(g):
    kept = jnp.where(own_lanes(), g, 0.0)
    return jnp.concatenate(
        [jnp.sum(kept[:8], axis=0, keepdims=True), jnp.sum(kept[8:], axis=0, keepdims=True)], axis=0
    )


def from_rows(rows):
    top = jnp.broadcast_to(rows[0:1], (8, D))
    low = jnp.broadcast_to(rows[1:2], (8, D))
    return spread_sum(jnp.where(own_lanes(), jnp.concatenate([top, low], axis=0), 0.0))


def diagonals():
    lane = iota((S, D), 1)
    return iota((S, D), 0) == (lane % S + lane // S) % S


def opposite():
    return (iota((S, D), 0) == iota((S, D), 1) + S // 2) & (iota((S, D), 1) < S // 2)


def pack_symmetric(g):
    return [
        jnp.sum(jnp.where(keep, g, 0.0), axis=0, keepdims=True) for keep in (diagonals(), opposite())
    ]


def from_symmetric(row, rest, ref):
    lower = jnp.where(diagonals(), jnp.broadcast_to(row, (S, D)), 0.0)
    ref[...] = spread_sum(lower + jnp.where(opposite(), jnp.broadcast_to(rest, (S, D)), 0.0))
    middle = iota((S, D), 0) == iota((S, D), 1) % S
    ref[...] = ref[...] + jnp.where(middle, 0.0, small_t(ref[...]))


def stack8(g):
    return jnp.concatenate([g] * 8, axis=0)


def small_mul(left, right):
    return exact(jnp.where(iota((S, D), 1) < S, left, 0.0), stack8(right))


def small_t(g):
    return stack8(g).T[:S]


def gram(left, right):
    return lax.dot_general(
        left, right, NT, precision=lax.Precision.HIGHEST, preferred_element_type=F32
    )


def widen(g):
    return jnp.concatenate([g] * 8, axis=1)


def mixed(coeffs, rows):
    return exact(small_t(coeffs)[:, :S], rows)


def gauss_solve(matrix, rhs):
    lane = iota((S, D), 1)
    row = iota((S, D), 0)
    work = jnp.where(lane < S, matrix, rhs)
    for pivot in range(S):
        row_new = work[pivot : pivot + 1] * (1.0 / work[pivot : pivot + 1, pivot : pivot + 1])
        factor = jnp.where(row == pivot, 0.0, work[:, pivot : pivot + 1])
        work = jnp.where(row == pivot, row_new, work - factor * row_new)
    return spread_sum(jnp.where((lane >= S) & (lane < 2 * S), work, 0.0))


def split(x):
    high = x.astype(BF16)
    return high, (x - high.astype(F32)).astype(BF16)


def stage_kernel(list_ref, tiles_ref, high_ref, low_ref, held, high, low, in_sems, out_sems):
    def fetch(i):
        rows = pl.ds(i % PIECES * PIECE, PIECE)
        return pltpu.make_async_copy(tiles_ref.at[i // PIECES, rows], held.at[i], in_sems.at[i])

    def flush(i):
        rows = pl.ds(i % PIECES * PIECE, PIECE)
        return [
            pltpu.make_async_copy(here.at[i], there.at[i // PIECES, rows], out_sems.at[which, i])
            for which, (here, there) in enumerate(((high, high_ref), (low, low_ref)))
        ]

    for i in range(4 * PIECES):
        fetch(i).start()
    for i in range(4 * PIECES):
        fetch(i).wait()
        tile, first = i // PIECES, i % PIECES * PIECE
        high[i], low[i] = split(held[i])

        @pl.when(list_ref[0, tile] == list_ref[1, tile])
        def _():
            row, col = iota((PIECE, B), 0) + first, iota((PIECE, B), 1)
            kept = jnp.where(row > col, held[i], jnp.where(row == col, 0.5 * held[i], 0.0))
            high[i], low[i] = split(kept)

        for copy in flush(i):
            copy.start()
    for i in range(4 * PIECES):
        for copy in flush(i):
            copy.wait()


def stage(tiles, tile_list):
    anywhere = pl.BlockSpec(memory_space=pltpu.HBM)
    return pl.pallas_call(
        stage_kernel,
        out_shape=[pltpu.HBM((4, B, B), BF16)] * 2,
        in_specs=[pl.BlockSpec(memory_space=pltpu.SMEM), anywhere],
        out_specs=[anywhere] * 2,
        scratch_shapes=[
            pltpu.VMEM((4 * PIECES, PIECE, B), F32),
            pltpu.VMEM((4 * PIECES, PIECE, B), BF16),
            pltpu.VMEM((4 * PIECES, PIECE, B), BF16),
            pltpu.SemaphoreType.DMA((4 * PIECES,)),
            pltpu.SemaphoreType.DMA((2, 4 * PIECES)),
        ],
        compiler_params=pltpu.CompilerParams(vmem_limit_bytes=40 << 20),
        name="stage",
    )(tile_list, tiles)


def by_core(mine, other):
    first = lax.axis_index("core") == 0
    return jnp.where(first, mine, other), jnp.where(first, other, mine)


def block_of(mine_ref, other_ref, block):
    field = []
    for half in range(2):
        chip = 2 * block + half
        for piece in by_core(mine_ref[chip], other_ref[chip]):
            field += [piece[:, :D], piece[:, D:]]
    return jnp.concatenate(field, axis=1)


def fetch_parts(high_hbm, low_hbm, high_ref, low_ref, sems):
    def fetch(i):
        tile, first, rows = PARTS[i]
        part = (tile, pl.ds(first, rows))
        return [
            pltpu.make_async_copy(there.at[part], here.at[part], sems.at[which, i])
            for which, (there, here) in enumerate(((high_hbm, high_ref), (low_hbm, low_ref)))
        ]

    for i in range(len(PARTS)):
        for copy in fetch(i):
            copy.start()
    return fetch


def multiply(fetch, high_ref, low_ref, field, put):
    def product(vec, tile, part, dims):
        vec_high, vec_low = split(vec)
        both = jnp.concatenate([vec_high, vec_low], axis=0)
        main = lax.dot_general(both, high_ref[tile, part], dims, preferred_element_type=F32)
        rest = lax.dot_general(vec_high, low_ref[tile, part], dims, preferred_element_type=F32)
        return main[:S] + (main[S:] + rest)

    half = jnp.zeros((S, S), F32)
    for tile in range(4):
        from_row, from_col = field(2 * tile), field(2 * tile + 1)
        into_row, into_col = [], []
        for i, (owner, first, rows) in enumerate(PARTS):
            if owner != tile:
                continue
            for copy in fetch(i):
                copy.wait()
            at = slice(first, first + rows)
            into_row.append(product(from_col, tile, at, NT))
            into_col.append(product(from_row[:, at], tile, at, NN))
        into_row = jnp.concatenate(into_row, axis=1)
        put(2 * tile, into_row)
        put(2 * tile + 1, sum(into_col[1:], into_col[0]))
        half = half + gram(from_row, into_row)
    return half + half.T


def first_kernel(
    list_ref, mine_ref, other_ref, right_ref, ridge_ref, high_hbm, low_hbm, out_ref,
    high_ref, low_ref, gram_ref, own_ref, sems,
):
    fetch = fetch_parts(high_hbm, low_hbm, high_ref, low_ref, sems)

    def field(k):
        return block_of(mine_ref, other_ref, list_ref[k % 2, k // 2])

    def put(k, value):
        tall = jnp.concatenate([value[:, j * D : (j + 1) * D] for j in range(J)], axis=0)
        out_ref[pl.ds(k, D, stride=R1_ROWS), :] = tall.T

    right = right_ref[...]
    scaled = jnp.concatenate([ridge_ref[0:1], ridge_ref[1:2]], axis=1) * right
    gram_ref[...] = gram(right, scaled)
    slot = iota((ENDS, D), 0)
    ends = jnp.zeros((ENDS, D), F32)
    for k in range(ENDS):
        ends = jnp.where(slot == k, list_ref[k % 2, k // 2].astype(F32), ends)
    own = [scaled[:, :D], scaled[:, D:], ends, jnp.zeros((D - 2 * S - ENDS, D), F32)]
    own_ref[...] = jnp.concatenate(own, axis=0).T
    curvature = multiply(fetch, high_ref, low_ref, field, put)
    row, rest = pack_symmetric(widen(gram_ref[...] + curvature))
    out_ref[pl.ds(ENDS, D, stride=R1_ROWS), :] = jnp.broadcast_to(row, (D, D))
    rest = jnp.concatenate([jnp.zeros((1, REST), F32), rest[:, : D - REST]], axis=1)
    out_ref[pl.ds(OWN, D, stride=R1_ROWS), :] = own_ref[...] + rest


def end_matches(ends, k):
    return ends[:, k : k + 1] == iota((D, NB), 1).astype(F32)


def select(matches, values):
    high, rest = split(values)
    low = (values - high.astype(F32) - rest.astype(F32)).astype(BF16)
    parts = jnp.dot(
        matches.astype(F32).astype(BF16),
        jnp.concatenate([high, rest, low], axis=1),
        preferred_element_type=F32,
    )
    return parts[:, :D] + parts[:, D : 2 * D] + parts[:, 2 * D :]


def owner_kernel(got_ref, out_ref):
    own = [got_ref[pl.ds(R1_ROWS * q + OWN, NB, stride=4 * R1_ROWS), :] for q in range(4)]
    total = jnp.concatenate([part[:, : 2 * S] for part in own], axis=1)
    ends = got_ref[pl.ds(OWN, D, stride=R1_ROWS), :][:, 2 * S : 2 * S + ENDS]
    for k in range(ENDS):
        part = got_ref[pl.ds(k, D, stride=R1_ROWS), :]
        total = total + select(end_matches(ends, k).astype(F32).T, part)
    for k in range(ENDS):
        out_ref[pl.ds(k, D, stride=G2_ROWS), :] = select(end_matches(ends, k), total)
    for q in range(4):
        own = [total[:, 2 * S * q : 2 * S * (q + 1)], jnp.zeros((NB, D - 2 * S), F32)]
        out_ref[pl.ds(G2_ROWS * q + ENDS, NB, stride=4 * G2_ROWS), :] = jnp.concatenate(own, axis=1)


def alpha_kernel(got_ref, mine_ref, other_ref, out_ref, norm_ref):
    norm_ref[...] = jnp.zeros((S, S), F32)
    for ref in (mine_ref, other_ref):

        @pl.loop(0, N, step=4)
        def _(chip):
            pieces = [ref[chip + i] for i in range(4)]
            wide = jnp.concatenate(pieces, axis=1)
            norm_ref[...] += gram(wide, wide)

    row, rest = [
        jnp.sum(got_ref[pl.ds(at, D, stride=R1_ROWS), :], axis=0, keepdims=True)
        for at in (ENDS, OWN)
    ]
    rest = jnp.concatenate([rest[:, REST:], jnp.zeros((1, REST), F32)], axis=1)
    out_ref[0] = widen(norm_ref[...])
    from_symmetric(row, rest, out_ref.at[1])
    out_ref[2] = gauss_solve(out_ref[1], out_ref[0])


def second_kernel(
    list_ref, mine_ref, other_ref, right_ref, ridge_ref, got_ref, small_ref, high_hbm, low_hbm,
    out_ref, keep_ref, high_ref, low_ref, gram_ref, sems,
):
    fetch = fetch_parts(high_hbm, low_hbm, high_ref, low_ref, sems)
    alpha_t = small_t(small_ref[2])[:, :S]

    def field(k):
        turned = got_ref[pl.ds(k, D, stride=G2_ROWS), :].T
        image = jnp.concatenate([turned[j * S : (j + 1) * S] for j in range(J)], axis=1)
        return block_of(mine_ref, other_ref, list_ref[k % 2, k // 2]) - exact(alpha_t, image)

    core = lax.axis_index("core")
    out_ref[...] = jnp.zeros(out_ref.shape, F32)

    def put(k, value):
        block = list_ref[k % 2, k // 2]
        for q in range(4):
            chip, side = 2 * block + q // 2, (q % 2 + core) % 2
            for j in range(2):
                rows = slice(j * S, (j + 1) * S)
                lanes = slice((2 * q + j) * D, (2 * q + j + 1) * D)
                out_ref[side, chip, rows] = out_ref[side, chip, rows] + value[:, lanes]

    right = right_ref[...]
    ridge = jnp.concatenate([ridge_ref[0:1], ridge_ref[1:2]], axis=1)
    turned = got_ref[pl.ds(ENDS, D, stride=G2_ROWS), :].T
    image = jnp.concatenate([turned[:S], turned[S : 2 * S]], axis=1)
    residual = right - exact(alpha_t, image)
    keep_ref[0] = residual
    keep_ref[1] = image
    gram_ref[0] = gram(residual, residual)
    gram_ref[1] = gram(residual, image)
    gram_ref[2] = gram(residual, ridge * residual)
    gram_ref[2] += multiply(fetch, high_ref, low_ref, field, put)
    flat = jnp.concatenate(
        [flat_rows(widen(gram_ref[i])) for i in range(3)] + [jnp.zeros((2, D), F32)], axis=0
    )
    for side in range(2):
        for chip in range(N):
            out_ref[side, chip, GRAMS:] = flat


def inverse_kernel(small_ref, right_ref, inverse_ref, begun_ref):
    unit = (iota((S, D), 0) == iota((S, D), 1) % S).astype(F32)
    inverse_ref[...] = gauss_solve(small_ref[0], unit)
    begun_ref[...] = mixed(small_ref[2], right_ref[...])


def last_kernel(
    got_ref, right_ref, ridge_ref, keep_ref, small_ref, inverse_ref, begun_ref,
    solution_ref, residual_ref, gram_ref,
):
    total = got_ref[0]
    for chip in range(1, N):
        total = total + got_ref[chip]
    right = right_ref[...]
    residual, image = keep_ref[0], keep_ref[1]
    ridge = jnp.concatenate([ridge_ref[0:1], ridge_ref[1:2]], axis=1)
    second = jnp.concatenate([total[:S], total[S : 2 * S]], axis=1) + ridge * residual
    for i in range(3):
        gram_ref[i] = from_rows(total[GRAMS + 2 * i : GRAMS + 2 * i + 2])
    gram_ref[5] = small_mul(inverse_ref[...], gram_ref[0])
    beta = gram_ref[5]
    gram_ref[3] = small_mul(gram_ref[1], beta)
    gram_ref[4] = small_mul(small_t(beta), small_mul(small_ref[1], beta))
    bent = gram_ref[2] + gram_ref[3] + small_t(gram_ref[3]) + gram_ref[4]
    last = gauss_solve(bent, gram_ref[0])
    direction = residual + mixed(beta, right)
    image_next = second + mixed(beta, image)
    solution_ref[...] = begun_ref[...] + mixed(last, direction)
    residual_ref[...] = residual - mixed(last, image_next)


HERE = pl.BlockSpec(memory_space=pltpu.VMEM)
SCALARS = pl.BlockSpec(memory_space=pltpu.SMEM)
THERE = pl.BlockSpec(memory_space=pltpu.HBM)
STAGED = [
    pltpu.VMEM((4, B, B), BF16),
    pltpu.VMEM((4, B, B), BF16),
]


def call(kernel, name, shapes, specs, args, scratch=(), limit=32):
    return pl.pallas_call(
        kernel,
        out_shape=[jax.ShapeDtypeStruct(shape, F32) for shape in shapes],
        in_specs=specs,
        out_specs=[HERE] * len(shapes),
        scratch_shapes=scratch,
        compiler_params=pltpu.CompilerParams(vmem_limit_bytes=limit << 20),
        name=name,
    )(*args)


def exchange_rows(x, rows):
    return lax.all_to_all(x.reshape(D, 1, rows * D), ALL, 0, 0).reshape(D * rows, D)


def swap(x):
    return lax.ppermute(x, "core", [(0, 1), (1, 0)])


def local(right, ridge, tiles, tile_list):
    ridge = ridge.reshape(2, D)
    tile_list = tile_list.T
    packed = jnp.broadcast_to(right, (N, S, 2 * D))
    later_list, packed = lax.optimization_barrier((tile_list, packed))
    staged = stage(tiles, later_list)
    mine = lax.all_to_all(packed, CHIPS, 0, 0)
    mine, *staged = lax.optimization_barrier((mine, *staged))
    other = swap(mine)
    sems = pltpu.SemaphoreType.DMA((2, len(PARTS)))
    (sent,) = call(
        first_kernel,
        "first",
        [(D * R1_ROWS, D)],
        [SCALARS] + [HERE] * 4 + [THERE] * 2,
        (tile_list, mine, other, right, ridge, *staged),
        [*STAGED, pltpu.VMEM((S, S), F32), pltpu.VMEM((D, D), F32), sems],
        48,
    )
    got = exchange_rows(sent, R1_ROWS)
    (sent,) = call(
        owner_kernel,
        "owner",
        [(D * G2_ROWS, D)],
        [HERE],
        (got,),
    )
    (small,) = call(
        alpha_kernel,
        "alpha",
        [(3, S, D)],
        [HERE] * 3,
        (got, mine, other),
        [pltpu.VMEM((S, S), F32)],
    )
    got = exchange_rows(sent, G2_ROWS)
    sent, keep = call(
        second_kernel,
        "second",
        [(2, N, SLOT, D), (2, S, 2 * D)],
        [SCALARS] + [HERE] * 6 + [THERE] * 2,
        (tile_list, mine, other, right, ridge, got, small, *staged),
        [*STAGED, pltpu.VMEM((3, S, S), F32), sems],
        48,
    )
    sent = sent[0] + swap(sent[1])
    later, sent = lax.optimization_barrier((small, sent))
    inverse, begun = call(
        inverse_kernel, "inverse", [(S, D), (S, 2 * D)], [HERE] * 2, (later, right)
    )
    got = lax.all_to_all(sent, CHIPS, 0, 0)
    got, inverse, begun = lax.optimization_barrier((got, inverse, begun))
    return tuple(
        call(
            last_kernel,
            "last",
            [(S, 2 * D)] * 2,
            [HERE] * 7,
            (got, right, ridge, keep, small, inverse, begun),
            [pltpu.VMEM((6, S, D), F32)],
        )
    )


def solution(mesh):
    mesh = jax.sharding.Mesh(mesh.devices.reshape(4, 16, 2), ALL)
    return jax.shard_map(
        local,
        mesh=mesh,
        in_specs=(P(None, ALL), P(ALL), P(ALL, None, None), P(ALL, None)),
        out_specs=(P(None, ALL), P(None, ALL)),
        check_vma=False,
    )
```

```python
import functools

import jax
import jax.numpy as jnp
from jax import lax
from jax.experimental import pallas as pl
from jax.experimental.pallas import tpu as pltpu
from jax.sharding import PartitionSpec as P

CHIPS = ("grp", "ring")
ALL = ("grp", "ring", "core")
OWNERS = ("core", "grp", "ring")
S = 16
B = 1024
NB = 32
D = 128
N = 64
J = 8
ENDS = 8
REST = 64
OWN = 9
SLOT = 40
GRAMS = 32
R1_ROWS = 10
G2_ROWS = 9
F32 = jnp.float32
BF16 = jnp.bfloat16
PIECE = 256
PIECES = B // PIECE
PARTS = [(0, 0, 256), (0, 256, 256), (0, 512, 512)]
PARTS += [(tile, first, 512) for tile in range(1, 4) for first in (0, 512)]
NT = (((1,), (1,)), ((), ()))
NN = (((1,), (0,)), ((), ()))


def iota(shape, dim):
    return lax.broadcasted_iota(jnp.int32, shape, dim)


def exact(left, right):
    return jnp.dot(left, right, precision=lax.Precision.HIGHEST, preferred_element_type=F32)


def same_column():
    return (iota((D, D), 0) % S == iota((D, D), 1) % S).astype(F32)


def spread_sum(x):
    return exact(x, same_column())


def own_lanes():
    return iota((S, D), 1) // S == iota((S, D), 0) % 8


def flat_rows(g):
    kept = jnp.where(own_lanes(), g, 0.0)
    return jnp.concatenate(
        [jnp.sum(kept[:8], axis=0, keepdims=True), jnp.sum(kept[8:], axis=0, keepdims=True)], axis=0
    )


def from_rows(rows):
    top = jnp.broadcast_to(rows[0:1], (8, D))
    low = jnp.broadcast_to(rows[1:2], (8, D))
    return spread_sum(jnp.where(own_lanes(), jnp.concatenate([top, low], axis=0), 0.0))


def diagonals():
    lane = iota((S, D), 1)
    return iota((S, D), 0) == (lane % S + lane // S) % S


def opposite():
    return (iota((S, D), 0) == iota((S, D), 1) + S // 2) & (iota((S, D), 1) < S // 2)


def pack_symmetric(g):
    return [
        jnp.sum(jnp.where(keep, g, 0.0), axis=0, keepdims=True) for keep in (diagonals(), opposite())
    ]


def from_symmetric(row, rest, ref):
    lower = jnp.where(diagonals(), jnp.broadcast_to(row, (S, D)), 0.0)
    ref[...] = spread_sum(lower + jnp.where(opposite(), jnp.broadcast_to(rest, (S, D)), 0.0))
    middle = iota((S, D), 0) == iota((S, D), 1) % S
    ref[...] = ref[...] + jnp.where(middle, 0.0, small_t(ref[...]))


def stack8(g):
    return jnp.concatenate([g] * 8, axis=0)


def small_mul(left, right):
    return exact(jnp.where(iota((S, D), 1) < S, left, 0.0), stack8(right))


def small_t(g):
    return stack8(g).T[:S]


def gram(left, right):
    return lax.dot_general(
        left, right, NT, precision=lax.Precision.HIGHEST, preferred_element_type=F32
    )


def widen(g):
    return jnp.concatenate([g] * 8, axis=1)


def mixed(coeffs, rows):
    return exact(small_t(coeffs)[:, :S], rows)


def gauss_solve(matrix, rhs):
    lane = iota((S, D), 1)
    row = iota((S, D), 0)
    work = jnp.where(lane < S, matrix, rhs)
    for pivot in range(S):
        row_new = work[pivot : pivot + 1] * (1.0 / work[pivot : pivot + 1, pivot : pivot + 1])
        factor = jnp.where(row == pivot, 0.0, work[:, pivot : pivot + 1])
        work = jnp.where(row == pivot, row_new, work - factor * row_new)
    return spread_sum(jnp.where((lane >= S) & (lane < 2 * S), work, 0.0))


def split(x):
    high = x.astype(BF16)
    return high, (x - high.astype(F32)).astype(BF16)


def stage_kernel(list_ref, tiles_ref, high_ref, low_ref, held, high, low, in_sems, out_sems):
    def fetch(i):
        rows = pl.ds(i % PIECES * PIECE, PIECE)
        return pltpu.make_async_copy(tiles_ref.at[i // PIECES, rows], held.at[i], in_sems.at[i])

    def flush(i):
        rows = pl.ds(i % PIECES * PIECE, PIECE)
        return [
            pltpu.make_async_copy(here.at[i], there.at[i // PIECES, rows], out_sems.at[which, i])
            for which, (here, there) in enumerate(((high, high_ref), (low, low_ref)))
        ]

    for i in range(4 * PIECES):
        fetch(i).start()
    for i in range(4 * PIECES):
        fetch(i).wait()
        tile, first = i // PIECES, i % PIECES * PIECE
        high[i], low[i] = split(held[i])

        @pl.when(list_ref[0, tile] == list_ref[1, tile])
        def _():
            row, col = iota((PIECE, B), 0) + first, iota((PIECE, B), 1)
            kept = jnp.where(row > col, held[i], jnp.where(row == col, 0.5 * held[i], 0.0))
            high[i], low[i] = split(kept)

        for copy in flush(i):
            copy.start()
    for i in range(4 * PIECES):
        for copy in flush(i):
            copy.wait()


def stage(tiles, tile_list):
    anywhere = pl.BlockSpec(memory_space=pltpu.HBM)
    return pl.pallas_call(
        stage_kernel,
        out_shape=[pltpu.HBM((4, B, B), BF16)] * 2,
        in_specs=[pl.BlockSpec(memory_space=pltpu.SMEM), anywhere],
        out_specs=[anywhere] * 2,
        scratch_shapes=[
            pltpu.VMEM((4 * PIECES, PIECE, B), F32),
            pltpu.VMEM((4 * PIECES, PIECE, B), BF16),
            pltpu.VMEM((4 * PIECES, PIECE, B), BF16),
            pltpu.SemaphoreType.DMA((4 * PIECES,)),
            pltpu.SemaphoreType.DMA((2, 4 * PIECES)),
        ],
        compiler_params=pltpu.CompilerParams(vmem_limit_bytes=40 << 20),
        name="stage",
    )(tile_list, tiles)


def by_core(mine, other):
    first = lax.axis_index("core") == 0
    return jnp.where(first, mine, other), jnp.where(first, other, mine)


def block_of(mine_ref, other_ref, block):
    field = []
    for half in range(2):
        chip = 2 * block + half
        for piece in by_core(mine_ref[chip], other_ref[chip]):
            field += [piece[:, :D], piece[:, D:]]
    return jnp.concatenate(field, axis=1)


def fetch_parts(high_hbm, low_hbm, high_ref, low_ref, sems):
    def fetch(i):
        tile, first, rows = PARTS[i]
        part = (tile, pl.ds(first, rows))
        return [
            pltpu.make_async_copy(there.at[part], here.at[part], sems.at[which, i])
            for which, (there, here) in enumerate(((high_hbm, high_ref), (low_hbm, low_ref)))
        ]

    for i in range(len(PARTS)):
        for copy in fetch(i):
            copy.start()
    return fetch


def multiply(fetch, high_ref, low_ref, field, put):
    def product(vec, tile, part, dims):
        vec_high, vec_low = split(vec)
        both = jnp.concatenate([vec_high, vec_low], axis=0)
        main = lax.dot_general(both, high_ref[tile, part], dims, preferred_element_type=F32)
        rest = lax.dot_general(vec_high, low_ref[tile, part], dims, preferred_element_type=F32)
        return main[:S] + (main[S:] + rest)

    half = jnp.zeros((S, S), F32)
    for tile in range(4):
        from_row, from_col = field(2 * tile), field(2 * tile + 1)
        into_row, into_col = [], []
        for i, (owner, first, rows) in enumerate(PARTS):
            if owner != tile:
                continue
            for copy in fetch(i):
                copy.wait()
            at = slice(first, first + rows)
            into_row.append(product(from_col, tile, at, NT))
            into_col.append(product(from_row[:, at], tile, at, NN))
        into_row = jnp.concatenate(into_row, axis=1)
        put(2 * tile, into_row)
        put(2 * tile + 1, sum(into_col[1:], into_col[0]))
        half = half + gram(from_row, into_row)
    return half + half.T


def first_kernel(
    list_ref, mine_ref, other_ref, right_ref, ridge_ref, high_hbm, low_hbm, out_ref,
    high_ref, low_ref, gram_ref, own_ref, sems,
):
    fetch = fetch_parts(high_hbm, low_hbm, high_ref, low_ref, sems)

    def field(k):
        return block_of(mine_ref, other_ref, list_ref[k % 2, k // 2])

    def put(k, value):
        tall = jnp.concatenate([value[:, j * D : (j + 1) * D] for j in range(J)], axis=0)
        out_ref[pl.ds(k, D, stride=R1_ROWS), :] = tall.T

    right = right_ref[...]
    scaled = jnp.concatenate([ridge_ref[0:1], ridge_ref[1:2]], axis=1) * right
    gram_ref[...] = gram(right, scaled)
    slot = iota((ENDS, D), 0)
    ends = jnp.zeros((ENDS, D), F32)
    for k in range(ENDS):
        ends = jnp.where(slot == k, list_ref[k % 2, k // 2].astype(F32), ends)
    own = [scaled[:, :D], scaled[:, D:], ends, jnp.zeros((D - 2 * S - ENDS, D), F32)]
    own_ref[...] = jnp.concatenate(own, axis=0).T
    curvature = multiply(fetch, high_ref, low_ref, field, put)
    row, rest = pack_symmetric(widen(gram_ref[...] + curvature))
    out_ref[pl.ds(ENDS, D, stride=R1_ROWS), :] = jnp.broadcast_to(row, (D, D))
    rest = jnp.concatenate([jnp.zeros((1, REST), F32), rest[:, : D - REST]], axis=1)
    out_ref[pl.ds(OWN, D, stride=R1_ROWS), :] = own_ref[...] + rest


def end_matches(ends, k):
    return ends[:, k : k + 1] == iota((D, NB), 1).astype(F32)


def select(matches, values):
    high, rest = split(values)
    low = (values - high.astype(F32) - rest.astype(F32)).astype(BF16)
    parts = jnp.dot(
        matches.astype(F32).astype(BF16),
        jnp.concatenate([high, rest, low], axis=1),
        preferred_element_type=F32,
    )
    return parts[:, :D] + parts[:, D : 2 * D] + parts[:, 2 * D :]


def quarter_owners(q, rows, row):
    return pl.ds(rows * (q % 2 * N + q // 2) + row, NB, stride=2 * rows)


def owner_kernel(got_ref, out_ref):
    own = [got_ref[quarter_owners(q, R1_ROWS, OWN), :] for q in range(4)]
    total = jnp.concatenate([part[:, : 2 * S] for part in own], axis=1)
    ends = got_ref[pl.ds(OWN, D, stride=R1_ROWS), :][:, 2 * S : 2 * S + ENDS]
    for k in range(ENDS):
        part = got_ref[pl.ds(k, D, stride=R1_ROWS), :]
        total = total + select(end_matches(ends, k).astype(F32).T, part)
    for k in range(ENDS):
        out_ref[pl.ds(k, D, stride=G2_ROWS), :] = select(end_matches(ends, k), total)
    for q in range(4):
        own = [total[:, 2 * S * q : 2 * S * (q + 1)], jnp.zeros((NB, D - 2 * S), F32)]
        out_ref[quarter_owners(q, G2_ROWS, ENDS), :] = jnp.concatenate(own, axis=1)


def norm_kernel(mine_ref, other_ref, out_ref, norm_ref):
    norm_ref[...] = jnp.zeros((S, S), F32)
    for ref in (mine_ref, other_ref):

        @pl.loop(0, N, step=4)
        def _(chip):
            wide = jnp.concatenate([ref[chip + i] for i in range(4)], axis=1)
            norm_ref[...] += gram(wide, wide)

    unit = (iota((S, D), 0) == iota((S, D), 1) % S).astype(F32)
    out_ref[0] = widen(norm_ref[...])
    out_ref[1] = gauss_solve(out_ref[0], unit)


def alpha_kernel(got_ref, norm_ref, right_ref, out_ref, begun_ref):
    row, rest = [
        jnp.sum(got_ref[pl.ds(at, D, stride=R1_ROWS), :], axis=0, keepdims=True)
        for at in (ENDS, OWN)
    ]
    rest = jnp.concatenate([rest[:, REST:], jnp.zeros((1, REST), F32)], axis=1)
    from_symmetric(row, rest, out_ref.at[0])
    out_ref[1] = gauss_solve(out_ref[0], norm_ref[0])
    begun_ref[...] = mixed(out_ref[1], right_ref[...])


def second_kernel(
    list_ref, mine_ref, other_ref, right_ref, ridge_ref, got_ref, small_ref, high_hbm, low_hbm,
    out_ref, keep_ref, high_ref, low_ref, gram_ref, sems,
):
    fetch = fetch_parts(high_hbm, low_hbm, high_ref, low_ref, sems)
    alpha_t = small_t(small_ref[1])[:, :S]

    def field(k):
        turned = got_ref[pl.ds(k, D, stride=G2_ROWS), :].T
        image = jnp.concatenate([turned[j * S : (j + 1) * S] for j in range(J)], axis=1)
        return block_of(mine_ref, other_ref, list_ref[k % 2, k // 2]) - exact(alpha_t, image)

    core = lax.axis_index("core")
    out_ref[...] = jnp.zeros(out_ref.shape, F32)

    def put(k, value):
        block = list_ref[k % 2, k // 2]
        for q in range(4):
            chip, side = 2 * block + q // 2, (q % 2 + core) % 2
            for j in range(2):
                rows = slice(j * S, (j + 1) * S)
                lanes = slice((2 * q + j) * D, (2 * q + j + 1) * D)
                out_ref[side, chip, rows] = out_ref[side, chip, rows] + value[:, lanes]

    right = right_ref[...]
    ridge = jnp.concatenate([ridge_ref[0:1], ridge_ref[1:2]], axis=1)
    turned = got_ref[pl.ds(ENDS, D, stride=G2_ROWS), :].T
    image = jnp.concatenate([turned[:S], turned[S : 2 * S]], axis=1)
    residual = right - exact(alpha_t, image)
    keep_ref[0] = residual
    keep_ref[1] = image
    gram_ref[0] = gram(residual, residual)
    gram_ref[1] = gram(residual, image)
    gram_ref[2] = gram(residual, ridge * residual)
    gram_ref[2] += multiply(fetch, high_ref, low_ref, field, put)
    flat = jnp.concatenate(
        [flat_rows(widen(gram_ref[i])) for i in range(3)] + [jnp.zeros((2, D), F32)], axis=0
    )
    for side in range(2):
        for chip in range(N):
            out_ref[side, chip, GRAMS:] = flat


def last_kernel(
    got_ref, right_ref, ridge_ref, keep_ref, norm_ref, small_ref, begun_ref,
    solution_ref, residual_ref, gram_ref,
):
    total = got_ref[0]
    for chip in range(1, N):
        total = total + got_ref[chip]
    right = right_ref[...]
    residual, image = keep_ref[0], keep_ref[1]
    ridge = jnp.concatenate([ridge_ref[0:1], ridge_ref[1:2]], axis=1)
    second = jnp.concatenate([total[:S], total[S : 2 * S]], axis=1) + ridge * residual
    for i in range(3):
        gram_ref[i] = from_rows(total[GRAMS + 2 * i : GRAMS + 2 * i + 2])
    gram_ref[5] = small_mul(norm_ref[1], gram_ref[0])
    beta = gram_ref[5]
    gram_ref[3] = small_mul(gram_ref[1], beta)
    gram_ref[4] = small_mul(small_t(beta), small_mul(small_ref[0], beta))
    bent = gram_ref[2] + gram_ref[3] + small_t(gram_ref[3]) + gram_ref[4]
    last = gauss_solve(bent, gram_ref[0])
    direction = residual + mixed(beta, right)
    image_next = second + mixed(beta, image)
    solution_ref[...] = begun_ref[...] + mixed(last, direction)
    residual_ref[...] = residual - mixed(last, image_next)


HERE = pl.BlockSpec(memory_space=pltpu.VMEM)
SCALARS = pl.BlockSpec(memory_space=pltpu.SMEM)
THERE = pl.BlockSpec(memory_space=pltpu.HBM)
STAGED = [
    pltpu.VMEM((4, B, B), BF16),
    pltpu.VMEM((4, B, B), BF16),
]


def call(kernel, name, shapes, specs, args, scratch=(), limit=32):
    return pl.pallas_call(
        kernel,
        out_shape=[jax.ShapeDtypeStruct(shape, F32) for shape in shapes],
        in_specs=specs,
        out_specs=[HERE] * len(shapes),
        scratch_shapes=scratch,
        compiler_params=pltpu.CompilerParams(vmem_limit_bytes=limit << 20),
        name=name,
    )(*args)


def exchange_rows(x, rows):
    return lax.all_to_all(x.reshape(D, 1, rows * D), OWNERS, 0, 0).reshape(D * rows, D)


def swap(x):
    return lax.ppermute(x, "core", [(0, 1), (1, 0)])


def local(right, ridge, tiles, tile_list):
    ridge = ridge.reshape(2, D)
    tile_list = tile_list.T
    packed = jnp.broadcast_to(right, (N, S, 2 * D))
    later_list, packed = lax.optimization_barrier((tile_list, packed))
    staged = stage(tiles, later_list)
    mine = lax.all_to_all(packed, CHIPS, 0, 0)
    mine, *staged = lax.optimization_barrier((mine, *staged))
    other = swap(mine)
    sems = pltpu.SemaphoreType.DMA((2, len(PARTS)))
    (sent,) = call(
        first_kernel,
        "first",
        [(D * R1_ROWS, D)],
        [SCALARS] + [HERE] * 4 + [THERE] * 2,
        (tile_list, mine, other, right, ridge, *staged),
        [*STAGED, pltpu.VMEM((S, S), F32), pltpu.VMEM((D, D), F32), sems],
        48,
    )
    later_mine, sent = lax.optimization_barrier((mine, sent))
    (norm,) = call(
        norm_kernel,
        "norm",
        [(2, S, D)],
        [HERE] * 2,
        (later_mine, other),
        [pltpu.VMEM((S, S), F32)],
    )
    got = exchange_rows(sent, R1_ROWS)
    got, norm = lax.optimization_barrier((got, norm))
    (sent,) = call(
        owner_kernel,
        "owner",
        [(D * G2_ROWS, D)],
        [HERE],
        (got,),
    )
    small, begun = call(
        alpha_kernel, "alpha", [(2, S, D), (S, 2 * D)], [HERE] * 3, (got, norm, right)
    )
    got = exchange_rows(sent, G2_ROWS)
    sent, keep = call(
        second_kernel,
        "second",
        [(2, N, SLOT, D), (2, S, 2 * D)],
        [SCALARS] + [HERE] * 6 + [THERE] * 2,
        (tile_list, mine, other, right, ridge, got, small, *staged),
        [*STAGED, pltpu.VMEM((3, S, S), F32), sems],
        48,
    )
    got = lax.all_to_all(sent[0] + swap(sent[1]), CHIPS, 0, 0)
    return tuple(
        call(
            last_kernel,
            "last",
            [(S, 2 * D)] * 2,
            [HERE] * 7,
            (got, right, ridge, keep, norm, small, begun),
            [pltpu.VMEM((6, S, D), F32)],
        )
    )


def solution(mesh):
    mesh = jax.sharding.Mesh(mesh.devices.reshape(4, 16, 2), ALL)
    return jax.shard_map(
        local,
        mesh=mesh,
        in_specs=(P(None, ALL), P(ALL), P(ALL, None, None), P(ALL, None)),
        out_specs=(P(None, ALL), P(None, ALL)),
        check_vma=False,
    )
```

```python
import functools

import jax
import jax.numpy as jnp
from jax import lax
from jax.experimental import pallas as pl
from jax.experimental.pallas import tpu as pltpu
from jax.sharding import PartitionSpec as P

CHIPS = ("grp", "ring")
ALL = ("grp", "ring", "core")
OWNERS = ("core", "grp", "ring")
S = 16
B = 1024
NB = 32
D = 128
N = 64
J = 8
ENDS = 8
REST = 64
OWN = 9
SLOT = 36
GRAMS = 32
R1_ROWS = 10
G2_ROWS = 9
F32 = jnp.float32
BF16 = jnp.bfloat16
PIECE = 256
PIECES = B // PIECE
PARTS = [(0, 0, 256), (0, 256, 256), (0, 512, 512)]
PARTS += [(tile, first, 512) for tile in range(1, 4) for first in (0, 512)]
NT = (((1,), (1,)), ((), ()))
NN = (((1,), (0,)), ((), ()))


def iota(shape, dim):
    return lax.broadcasted_iota(jnp.int32, shape, dim)


def exact(left, right):
    return jnp.dot(left, right, precision=lax.Precision.HIGHEST, preferred_element_type=F32)


def same_column():
    return (iota((D, D), 0) % S == iota((D, D), 1) % S).astype(F32)


def spread_sum(x):
    return exact(x, same_column())


def own_lanes():
    return iota((S, D), 1) // S == iota((S, D), 0) % 8


def flat_rows(g):
    kept = jnp.where(own_lanes(), g, 0.0)
    return jnp.concatenate(
        [jnp.sum(kept[:8], axis=0, keepdims=True), jnp.sum(kept[8:], axis=0, keepdims=True)], axis=0
    )


def from_rows(rows):
    top = jnp.broadcast_to(rows[0:1], (8, D))
    low = jnp.broadcast_to(rows[1:2], (8, D))
    return spread_sum(jnp.where(own_lanes(), jnp.concatenate([top, low], axis=0), 0.0))


def diagonals():
    lane = iota((S, D), 1)
    return iota((S, D), 0) == (lane % S + lane // S) % S


def opposite():
    return (iota((S, D), 0) == iota((S, D), 1) + S // 2) & (iota((S, D), 1) < S // 2)


def pack_symmetric(g):
    return [
        jnp.sum(jnp.where(keep, g, 0.0), axis=0, keepdims=True) for keep in (diagonals(), opposite())
    ]


def from_symmetric(row, rest, ref):
    lower = jnp.where(diagonals(), jnp.broadcast_to(row, (S, D)), 0.0)
    ref[...] = spread_sum(lower + jnp.where(opposite(), jnp.broadcast_to(rest, (S, D)), 0.0))
    middle = iota((S, D), 0) == iota((S, D), 1) % S
    ref[...] = ref[...] + jnp.where(middle, 0.0, small_t(ref[...]))


def stack8(g):
    return jnp.concatenate([g] * 8, axis=0)


def small_mul(left, right):
    return exact(jnp.where(iota((S, D), 1) < S, left, 0.0), stack8(right))


def small_t(g):
    return stack8(g).T[:S]


def gram(left, right):
    return lax.dot_general(
        left, right, NT, precision=lax.Precision.HIGHEST, preferred_element_type=F32
    )


def widen(g):
    return jnp.concatenate([g] * 8, axis=1)


def mixed(coeffs, rows):
    return exact(small_t(coeffs)[:, :S], rows)


def gauss_solve(matrix, rhs):
    lane = iota((S, D), 1)
    row = iota((S, D), 0)
    work = jnp.where(lane < S, matrix, rhs)
    for pivot in range(S):
        row_new = work[pivot : pivot + 1] * (1.0 / work[pivot : pivot + 1, pivot : pivot + 1])
        factor = jnp.where(row == pivot, 0.0, work[:, pivot : pivot + 1])
        work = jnp.where(row == pivot, row_new, work - factor * row_new)
    return spread_sum(jnp.where((lane >= S) & (lane < 2 * S), work, 0.0))


def split(x):
    high = x.astype(BF16)
    return high, (x - high.astype(F32)).astype(BF16)


def stage_kernel(list_ref, tiles_ref, high_ref, low_ref, held, high, low, in_sems, out_sems):
    def fetch(i):
        rows = pl.ds(i % PIECES * PIECE, PIECE)
        return pltpu.make_async_copy(tiles_ref.at[i // PIECES, rows], held.at[i], in_sems.at[i])

    def flush(i):
        rows = pl.ds(i % PIECES * PIECE, PIECE)
        return [
            pltpu.make_async_copy(here.at[i], there.at[i // PIECES, rows], out_sems.at[which, i])
            for which, (here, there) in enumerate(((high, high_ref), (low, low_ref)))
        ]

    for i in range(4 * PIECES):
        fetch(i).start()
    for i in range(4 * PIECES):
        fetch(i).wait()
        tile, first = i // PIECES, i % PIECES * PIECE
        high[i], low[i] = split(held[i])

        @pl.when(list_ref[0, tile] == list_ref[1, tile])
        def _():
            row, col = iota((PIECE, B), 0) + first, iota((PIECE, B), 1)
            kept = jnp.where(row > col, held[i], jnp.where(row == col, 0.5 * held[i], 0.0))
            high[i], low[i] = split(kept)

        for copy in flush(i):
            copy.start()
    for i in range(4 * PIECES):
        for copy in flush(i):
            copy.wait()


def stage(tiles, tile_list):
    anywhere = pl.BlockSpec(memory_space=pltpu.HBM)
    return pl.pallas_call(
        stage_kernel,
        out_shape=[pltpu.HBM((4, B, B), BF16)] * 2,
        in_specs=[pl.BlockSpec(memory_space=pltpu.SMEM), anywhere],
        out_specs=[anywhere] * 2,
        scratch_shapes=[
            pltpu.VMEM((4 * PIECES, PIECE, B), F32),
            pltpu.VMEM((4 * PIECES, PIECE, B), BF16),
            pltpu.VMEM((4 * PIECES, PIECE, B), BF16),
            pltpu.SemaphoreType.DMA((4 * PIECES,)),
            pltpu.SemaphoreType.DMA((2, 4 * PIECES)),
        ],
        compiler_params=pltpu.CompilerParams(vmem_limit_bytes=40 << 20),
        name="stage",
    )(tile_list, tiles)


def by_core(mine, other):
    first = lax.axis_index("core") == 0
    return jnp.where(first, mine, other), jnp.where(first, other, mine)


def block_of(mine_ref, other_ref, block):
    field = []
    for half in range(2):
        chip = 2 * block + half
        for piece in by_core(mine_ref[chip], other_ref[chip]):
            field += [piece[:, :D], piece[:, D:]]
    return jnp.concatenate(field, axis=1)


def fetch_parts(high_hbm, low_hbm, high_ref, low_ref, sems):
    def fetch(i):
        tile, first, rows = PARTS[i]
        part = (tile, pl.ds(first, rows))
        return [
            pltpu.make_async_copy(there.at[part], here.at[part], sems.at[which, i])
            for which, (there, here) in enumerate(((high_hbm, high_ref), (low_hbm, low_ref)))
        ]

    for i in range(len(PARTS)):
        for copy in fetch(i):
            copy.start()
    return fetch


def multiply(fetch, high_ref, low_ref, field, put):
    def product(vec, tile, part, dims):
        vec_high, vec_low = split(vec)
        both = jnp.concatenate([vec_high, vec_low], axis=0)
        main = lax.dot_general(both, high_ref[tile, part], dims, preferred_element_type=F32)
        rest = lax.dot_general(vec_high, low_ref[tile, part], dims, preferred_element_type=F32)
        return main[:S] + (main[S:] + rest)

    half = jnp.zeros((S, S), F32)
    for tile in range(4):
        from_row, from_col = field(2 * tile), field(2 * tile + 1)
        into_row, into_col = [], []
        for i, (owner, first, rows) in enumerate(PARTS):
            if owner != tile:
                continue
            for copy in fetch(i):
                copy.wait()
            at = slice(first, first + rows)
            into_row.append(product(from_col, tile, at, NT))
            into_col.append(product(from_row[:, at], tile, at, NN))
        into_row = jnp.concatenate(into_row, axis=1)
        put(2 * tile, into_row)
        put(2 * tile + 1, sum(into_col[1:], into_col[0]))
        half = half + gram(from_row, into_row)
    return half + half.T


def first_kernel(
    list_ref, mine_ref, other_ref, right_ref, ridge_ref, high_hbm, low_hbm, out_ref,
    high_ref, low_ref, gram_ref, own_ref, sems,
):
    fetch = fetch_parts(high_hbm, low_hbm, high_ref, low_ref, sems)

    def field(k):
        return block_of(mine_ref, other_ref, list_ref[k % 2, k // 2])

    def put(k, value):
        tall = jnp.concatenate([value[:, j * D : (j + 1) * D] for j in range(J)], axis=0)
        out_ref[pl.ds(k, D, stride=R1_ROWS), :] = tall.T

    right = right_ref[...]
    scaled = jnp.concatenate([ridge_ref[0:1], ridge_ref[1:2]], axis=1) * right
    gram_ref[...] = gram(right, scaled)
    slot = iota((ENDS, D), 0)
    ends = jnp.zeros((ENDS, D), F32)
    for k in range(ENDS):
        ends = jnp.where(slot == k, list_ref[k % 2, k // 2].astype(F32), ends)
    own = [scaled[:, :D], scaled[:, D:], ends, jnp.zeros((D - 2 * S - ENDS, D), F32)]
    own_ref[...] = jnp.concatenate(own, axis=0).T
    curvature = multiply(fetch, high_ref, low_ref, field, put)
    row, rest = pack_symmetric(widen(gram_ref[...] + curvature))
    out_ref[pl.ds(ENDS, D, stride=R1_ROWS), :] = jnp.broadcast_to(row, (D, D))
    rest = jnp.concatenate([jnp.zeros((1, REST), F32), rest[:, : D - REST]], axis=1)
    out_ref[pl.ds(OWN, D, stride=R1_ROWS), :] = own_ref[...] + rest


def end_matches(ends, k):
    return ends[:, k : k + 1] == iota((D, NB), 1).astype(F32)


def select(matches, values):
    high, rest = split(values)
    low = (values - high.astype(F32) - rest.astype(F32)).astype(BF16)
    parts = jnp.dot(
        matches.astype(F32).astype(BF16),
        jnp.concatenate([high, rest, low], axis=1),
        preferred_element_type=F32,
    )
    return parts[:, :D] + parts[:, D : 2 * D] + parts[:, 2 * D :]


def quarter_owners(q, rows, row):
    return pl.ds(rows * (q % 2 * N + q // 2) + row, NB, stride=2 * rows)


def owner_kernel(got_ref, out_ref):
    own = [got_ref[quarter_owners(q, R1_ROWS, OWN), :] for q in range(4)]
    total = jnp.concatenate([part[:, : 2 * S] for part in own], axis=1)
    ends = got_ref[pl.ds(OWN, D, stride=R1_ROWS), :][:, 2 * S : 2 * S + ENDS]
    for k in range(ENDS):
        part = got_ref[pl.ds(k, D, stride=R1_ROWS), :]
        total = total + select(end_matches(ends, k).astype(F32).T, part)
    for k in range(ENDS):
        out_ref[pl.ds(k, D, stride=G2_ROWS), :] = select(end_matches(ends, k), total)
    for q in range(4):
        own = [total[:, 2 * S * q : 2 * S * (q + 1)], jnp.zeros((NB, D - 2 * S), F32)]
        out_ref[quarter_owners(q, G2_ROWS, ENDS), :] = jnp.concatenate(own, axis=1)


def norm_kernel(mine_ref, other_ref, out_ref, norm_ref):
    norm_ref[...] = jnp.zeros((3 * S, 3 * S), F32)
    for ref in (mine_ref, other_ref):

        @pl.loop(0, N, step=8)
        def _(chip):
            wide = jnp.concatenate([ref[chip + i] for i in range(8)], axis=1)
            high, rest = split(wide)
            low = (wide - high.astype(F32) - rest.astype(F32)).astype(BF16)
            parts = jnp.concatenate([high, rest, low], axis=0)
            norm_ref[...] += lax.dot_general(parts, parts, NT, preferred_element_type=F32)

    norm = norm_ref[...]
    norm = norm[:S] + norm[S : 2 * S] + norm[2 * S :]
    norm = norm[:, :S] + norm[:, S : 2 * S] + norm[:, 2 * S :]
    unit = (iota((S, D), 0) == iota((S, D), 1) % S).astype(F32)
    out_ref[0] = widen(norm)
    out_ref[1] = gauss_solve(out_ref[0], unit)


def alpha_kernel(got_ref, norm_ref, right_ref, out_ref, begun_ref):
    row, rest = [
        jnp.sum(got_ref[pl.ds(at, D, stride=R1_ROWS), :], axis=0, keepdims=True)
        for at in (ENDS, OWN)
    ]
    rest = jnp.concatenate([rest[:, REST:], jnp.zeros((1, REST), F32)], axis=1)
    from_symmetric(row, rest, out_ref.at[0])
    out_ref[1] = gauss_solve(out_ref[0], norm_ref[0])
    begun_ref[...] = mixed(out_ref[1], right_ref[...])


def second_kernel(
    list_ref, mine_ref, other_ref, right_ref, ridge_ref, got_ref, small_ref, high_hbm, low_hbm,
    out_ref, keep_ref, high_ref, low_ref, gram_ref, sems,
):
    fetch = fetch_parts(high_hbm, low_hbm, high_ref, low_ref, sems)
    alpha_t = small_t(small_ref[1])[:, :S]

    def field(k):
        turned = got_ref[pl.ds(k, D, stride=G2_ROWS), :].T
        image = jnp.concatenate([turned[j * S : (j + 1) * S] for j in range(J)], axis=1)
        return block_of(mine_ref, other_ref, list_ref[k % 2, k // 2]) - exact(alpha_t, image)

    core = lax.axis_index("core")
    out_ref[...] = jnp.zeros(out_ref.shape, F32)

    def put(k, value):
        block = list_ref[k % 2, k // 2]
        for q in range(4):
            chip, side = 2 * block + q // 2, (q % 2 + core) % 2
            for j in range(2):
                rows = pl.ds(chip * SLOT + j * S, S)
                lanes = slice((2 * q + j) * D, (2 * q + j + 1) * D)
                out_ref[side, rows, :] = out_ref[side, rows, :] + value[:, lanes]

    right = right_ref[...]
    ridge = jnp.concatenate([ridge_ref[0:1], ridge_ref[1:2]], axis=1)
    turned = got_ref[pl.ds(ENDS, D, stride=G2_ROWS), :].T
    image = jnp.concatenate([turned[:S], turned[S : 2 * S]], axis=1)
    residual = right - exact(alpha_t, image)
    keep_ref[0] = residual
    keep_ref[1] = image
    gram_ref[0] = gram(residual, residual)
    gram_ref[1] = gram(residual, ridge * residual)
    gram_ref[1] += multiply(fetch, high_ref, low_ref, field, put)
    flat = jnp.concatenate([flat_rows(widen(gram_ref[i])) for i in range(2)], axis=0)
    for side in range(2):
        for chip in range(N):
            out_ref[side, chip * SLOT + GRAMS : (chip + 1) * SLOT, :] = flat


def last_kernel(
    got_ref, right_ref, ridge_ref, keep_ref, norm_ref, small_ref, begun_ref,
    solution_ref, residual_ref, gram_ref,
):
    total = got_ref[: 2 * SLOT]
    for chip in range(2, N, 2):
        total = total + got_ref[chip * SLOT : (chip + 2) * SLOT]
    total = total[:SLOT] + total[SLOT:]
    right = right_ref[...]
    residual, image = keep_ref[0], keep_ref[1]
    ridge = jnp.concatenate([ridge_ref[0:1], ridge_ref[1:2]], axis=1)
    second = jnp.concatenate([total[:S], total[S : 2 * S]], axis=1) + ridge * residual
    for i in range(2):
        gram_ref[i] = from_rows(total[GRAMS + 2 * i : GRAMS + 2 * i + 2])
    gram_ref[2] = small_mul(norm_ref[1], gram_ref[0])
    beta = gram_ref[2]
    gram_ref[3] = small_mul(small_t(beta), small_mul(small_ref[0], beta))
    last = gauss_solve(gram_ref[1] - gram_ref[3], gram_ref[0])
    direction = residual + mixed(beta, right)
    image_next = second + mixed(beta, image)
    solution_ref[...] = begun_ref[...] + mixed(last, direction)
    residual_ref[...] = residual - mixed(last, image_next)


HERE = pl.BlockSpec(memory_space=pltpu.VMEM)
SCALARS = pl.BlockSpec(memory_space=pltpu.SMEM)
THERE = pl.BlockSpec(memory_space=pltpu.HBM)
STAGED = [
    pltpu.VMEM((4, B, B), BF16),
    pltpu.VMEM((4, B, B), BF16),
]


def call(kernel, name, shapes, specs, args, scratch=(), limit=32):
    return pl.pallas_call(
        kernel,
        out_shape=[jax.ShapeDtypeStruct(shape, F32) for shape in shapes],
        in_specs=specs,
        out_specs=[HERE] * len(shapes),
        scratch_shapes=scratch,
        compiler_params=pltpu.CompilerParams(vmem_limit_bytes=limit << 20),
        name=name,
    )(*args)


def exchange_rows(x, rows):
    return lax.all_to_all(x.reshape(D, 1, rows * D), OWNERS, 0, 0).reshape(D * rows, D)


def swap(x):
    return lax.ppermute(x, "core", [(0, 1), (1, 0)])


def local(right, ridge, tiles, tile_list):
    ridge = ridge.reshape(2, D)
    tile_list = tile_list.T
    packed = jnp.broadcast_to(right, (N, S, 2 * D))
    later_list, packed = lax.optimization_barrier((tile_list, packed))
    staged = stage(tiles, later_list)
    mine = lax.all_to_all(packed, CHIPS, 0, 0)
    mine, *staged = lax.optimization_barrier((mine, *staged))
    other = swap(mine)
    sems = pltpu.SemaphoreType.DMA((2, len(PARTS)))
    (sent,) = call(
        first_kernel,
        "first",
        [(D * R1_ROWS, D)],
        [SCALARS] + [HERE] * 4 + [THERE] * 2,
        (tile_list, mine, other, right, ridge, *staged),
        [*STAGED, pltpu.VMEM((S, S), F32), pltpu.VMEM((D, D), F32), sems],
        48,
    )
    got = exchange_rows(sent, R1_ROWS)
    (sent,) = call(
        owner_kernel,
        "owner",
        [(D * G2_ROWS, D)],
        [HERE],
        (got,),
    )
    later_mine, sent = lax.optimization_barrier((mine, sent))
    (norm,) = call(
        norm_kernel,
        "norm",
        [(2, S, D)],
        [HERE] * 2,
        (later_mine, other),
        [pltpu.VMEM((3 * S, 3 * S), F32)],
    )
    small, begun = call(
        alpha_kernel, "alpha", [(2, S, D), (S, 2 * D)], [HERE] * 3, (got, norm, right)
    )
    got = exchange_rows(sent, G2_ROWS)
    sent, keep = call(
        second_kernel,
        "second",
        [(2, N * SLOT, D), (2, S, 2 * D)],
        [SCALARS] + [HERE] * 6 + [THERE] * 2,
        (tile_list, mine, other, right, ridge, got, small, *staged),
        [*STAGED, pltpu.VMEM((2, S, S), F32), sems],
        48,
    )
    sent = (sent[0] + swap(sent[1])).reshape(N, 1, SLOT * D)
    got = lax.all_to_all(sent, CHIPS, 0, 0).reshape(N * SLOT, D)
    return tuple(
        call(
            last_kernel,
            "last",
            [(S, 2 * D)] * 2,
            [HERE] * 7,
            (got, right, ridge, keep, norm, small, begun),
            [pltpu.VMEM((4, S, D), F32)],
        )
    )


def solution(mesh):
    mesh = jax.sharding.Mesh(mesh.devices.reshape(4, 16, 2), ALL)
    return jax.shard_map(
        local,
        mesh=mesh,
        in_specs=(P(None, ALL), P(ALL), P(ALL, None, None), P(ALL, None)),
        out_specs=(P(None, ALL), P(None, ALL)),
        check_vma=False,
    )
```

```python
import functools

import jax
import jax.numpy as jnp
from jax import lax
from jax.experimental import pallas as pl
from jax.experimental.pallas import tpu as pltpu
from jax.sharding import PartitionSpec as P

CHIPS = ("grp", "ring")
ALL = ("grp", "ring", "core")
OWNERS = ("core", "grp", "ring")
S = 16
B = 1024
NB = 32
D = 128
N = 64
J = 8
ENDS = 8
REST = 64
OWN = 9
SLOT = 36
GRAMS = 32
R1_ROWS = 10
G2_ROWS = 9
F32 = jnp.float32
BF16 = jnp.bfloat16
PIECE = 256
PIECES = B // PIECE
PARTS = [(0, 0, 256), (0, 256, 256), (0, 512, 512), (1, 0, B), (2, 0, B), (3, 0, B)]
AHEAD = 4
NT = (((1,), (1,)), ((), ()))
NN = (((1,), (0,)), ((), ()))


def iota(shape, dim):
    return lax.broadcasted_iota(jnp.int32, shape, dim)


def exact(left, right):
    return jnp.dot(left, right, precision=lax.Precision.HIGHEST, preferred_element_type=F32)


def same_column():
    return (iota((D, D), 0) % S == iota((D, D), 1) % S).astype(F32)


def spread_sum(x):
    return exact(x, same_column())


def own_lanes():
    return iota((S, D), 1) // S == iota((S, D), 0) % 8


def flat_rows(g):
    kept = jnp.where(own_lanes(), g, 0.0)
    return jnp.concatenate(
        [jnp.sum(kept[:8], axis=0, keepdims=True), jnp.sum(kept[8:], axis=0, keepdims=True)], axis=0
    )


def from_rows(rows):
    top = jnp.broadcast_to(rows[0:1], (8, D))
    low = jnp.broadcast_to(rows[1:2], (8, D))
    return spread_sum(jnp.where(own_lanes(), jnp.concatenate([top, low], axis=0), 0.0))


def diagonals():
    lane = iota((S, D), 1)
    return iota((S, D), 0) == (lane % S + lane // S) % S


def opposite():
    return (iota((S, D), 0) == iota((S, D), 1) + S // 2) & (iota((S, D), 1) < S // 2)


def pack_symmetric(g):
    return [
        jnp.sum(jnp.where(keep, g, 0.0), axis=0, keepdims=True) for keep in (diagonals(), opposite())
    ]


def from_symmetric(row, rest, ref):
    lower = jnp.where(diagonals(), jnp.broadcast_to(row, (S, D)), 0.0)
    ref[...] = spread_sum(lower + jnp.where(opposite(), jnp.broadcast_to(rest, (S, D)), 0.0))
    middle = iota((S, D), 0) == iota((S, D), 1) % S
    ref[...] = ref[...] + jnp.where(middle, 0.0, small_t(ref[...]))


def stack8(g):
    return jnp.concatenate([g] * 8, axis=0)


def small_mul(left, right):
    return exact(jnp.where(iota((S, D), 1) < S, left, 0.0), stack8(right))


def small_t(g):
    return stack8(g).T[:S]


def gram(left, right):
    return lax.dot_general(
        left, right, NT, precision=lax.Precision.HIGHEST, preferred_element_type=F32
    )


def widen(g):
    return jnp.concatenate([g] * 8, axis=1)


def mixed(coeffs, rows):
    return exact(small_t(coeffs)[:, :S], rows)


def gauss_solve(matrix, rhs):
    lane = iota((S, D), 1)
    row = iota((S, D), 0)
    work = jnp.where(lane < S, matrix, rhs)
    for pivot in range(S):
        row_new = work[pivot : pivot + 1] * (1.0 / work[pivot : pivot + 1, pivot : pivot + 1])
        factor = jnp.where(row == pivot, 0.0, work[:, pivot : pivot + 1])
        work = jnp.where(row == pivot, row_new, work - factor * row_new)
    return spread_sum(jnp.where((lane >= S) & (lane < 2 * S), work, 0.0))


def split(x):
    high = x.astype(BF16)
    return high, (x - high.astype(F32)).astype(BF16)


def stage_kernel(list_ref, tiles_ref, high_ref, low_ref, held, high, low, in_sems, out_sems):
    def fetch(i):
        rows = pl.ds(i % PIECES * PIECE, PIECE)
        return pltpu.make_async_copy(tiles_ref.at[i // PIECES, rows], held.at[i], in_sems.at[i])

    def flush(i):
        rows = pl.ds(i % PIECES * PIECE, PIECE)
        return [
            pltpu.make_async_copy(here.at[i], there.at[i // PIECES, rows], out_sems.at[which, i])
            for which, (here, there) in enumerate(((high, high_ref), (low, low_ref)))
        ]

    for i in range(AHEAD):
        fetch(i).start()
    for i in range(4 * PIECES):
        fetch(i).wait()
        if i + AHEAD < 4 * PIECES:
            fetch(i + AHEAD).start()
        tile, first = i // PIECES, i % PIECES * PIECE
        high[i], low[i] = split(held[i])

        @pl.when(list_ref[0, tile] == list_ref[1, tile])
        def _():
            row, col = iota((PIECE, B), 0) + first, iota((PIECE, B), 1)
            kept = jnp.where(row > col, held[i], jnp.where(row == col, 0.5 * held[i], 0.0))
            high[i], low[i] = split(kept)

        for copy in flush(i):
            copy.start()
    for i in range(4 * PIECES):
        for copy in flush(i):
            copy.wait()


def stage(tiles, tile_list):
    anywhere = pl.BlockSpec(memory_space=pltpu.HBM)
    return pl.pallas_call(
        stage_kernel,
        out_shape=[pltpu.HBM((4, B, B), BF16)] * 2,
        in_specs=[pl.BlockSpec(memory_space=pltpu.SMEM), anywhere],
        out_specs=[anywhere] * 2,
        scratch_shapes=[
            pltpu.VMEM((4 * PIECES, PIECE, B), F32),
            pltpu.VMEM((4 * PIECES, PIECE, B), BF16),
            pltpu.VMEM((4 * PIECES, PIECE, B), BF16),
            pltpu.SemaphoreType.DMA((4 * PIECES,)),
            pltpu.SemaphoreType.DMA((2, 4 * PIECES)),
        ],
        compiler_params=pltpu.CompilerParams(vmem_limit_bytes=40 << 20),
        name="stage",
    )(tile_list, tiles)


def by_core(mine, other):
    first = lax.axis_index("core") == 0
    return jnp.where(first, mine, other), jnp.where(first, other, mine)


def block_of(mine_ref, other_ref, block):
    field = []
    for half in range(2):
        chip = 2 * block + half
        for piece in by_core(mine_ref[chip], other_ref[chip]):
            field += [piece[:, :D], piece[:, D:]]
    return jnp.concatenate(field, axis=1)


def fetch_parts(high_hbm, low_hbm, high_ref, low_ref, sems):
    def fetch(i):
        tile, first, rows = PARTS[i]
        part = (tile, pl.ds(first, rows))
        return [
            pltpu.make_async_copy(there.at[part], here.at[part], sems.at[which, i])
            for which, (there, here) in enumerate(((high_hbm, high_ref), (low_hbm, low_ref)))
        ]

    for i in range(len(PARTS)):
        for copy in fetch(i):
            copy.start()
    return fetch


def multiply(fetch, high_ref, low_ref, field, put):
    def product(vec, tile, part, dims):
        vec_high, vec_low = split(vec)
        both = jnp.concatenate([vec_high, vec_low], axis=0)
        main = lax.dot_general(both, high_ref[tile, part], dims, preferred_element_type=F32)
        rest = lax.dot_general(vec_high, low_ref[tile, part], dims, preferred_element_type=F32)
        return main[:S] + (main[S:] + rest)

    half = jnp.zeros((S, S), F32)
    for tile in range(4):
        from_row, from_col = field(2 * tile), field(2 * tile + 1)
        into_row, into_col = [], []
        for i, (owner, first, rows) in enumerate(PARTS):
            if owner != tile:
                continue
            for copy in fetch(i):
                copy.wait()
            at = slice(first, first + rows)
            into_row.append(product(from_col, tile, at, NT))
            into_col.append(product(from_row[:, at], tile, at, NN))
        into_row = jnp.concatenate(into_row, axis=1)
        put(2 * tile, into_row)
        put(2 * tile + 1, sum(into_col[1:], into_col[0]))
        half = half + gram(from_row, into_row)
    return half + half.T


def first_kernel(
    list_ref, mine_ref, other_ref, right_ref, ridge_ref, high_hbm, low_hbm, out_ref,
    high_ref, low_ref, gram_ref, own_ref, sems,
):
    fetch = fetch_parts(high_hbm, low_hbm, high_ref, low_ref, sems)

    def field(k):
        return block_of(mine_ref, other_ref, list_ref[k % 2, k // 2])

    def put(k, value):
        tall = jnp.concatenate([value[:, j * D : (j + 1) * D] for j in range(J)], axis=0)
        out_ref[pl.ds(k, D, stride=R1_ROWS), :] = tall.T

    right = right_ref[...]
    scaled = jnp.concatenate([ridge_ref[0:1], ridge_ref[1:2]], axis=1) * right
    gram_ref[...] = gram(right, scaled)
    slot = iota((ENDS, D), 0)
    ends = jnp.zeros((ENDS, D), F32)
    for k in range(ENDS):
        ends = jnp.where(slot == k, list_ref[k % 2, k // 2].astype(F32), ends)
    own = [scaled[:, :D], scaled[:, D:], ends, jnp.zeros((D - 2 * S - ENDS, D), F32)]
    own_ref[...] = jnp.concatenate(own, axis=0).T
    curvature = multiply(fetch, high_ref, low_ref, field, put)
    row, rest = pack_symmetric(widen(gram_ref[...] + curvature))
    out_ref[pl.ds(ENDS, D, stride=R1_ROWS), :] = jnp.broadcast_to(row, (D, D))
    rest = jnp.concatenate([jnp.zeros((1, REST), F32), rest[:, : D - REST]], axis=1)
    out_ref[pl.ds(OWN, D, stride=R1_ROWS), :] = own_ref[...] + rest


def end_matches(ends, k):
    return ends[:, k : k + 1] == iota((D, NB), 1).astype(F32)


def select(matches, values):
    high, rest = split(values)
    low = (values - high.astype(F32) - rest.astype(F32)).astype(BF16)
    parts = jnp.dot(
        matches.astype(F32).astype(BF16),
        jnp.concatenate([high, rest, low], axis=1),
        preferred_element_type=F32,
    )
    return parts[:, :D] + parts[:, D : 2 * D] + parts[:, 2 * D :]


def quarter_owners(q, rows, row):
    return pl.ds(rows * (q % 2 * N + q // 2) + row, NB, stride=2 * rows)


def owner_kernel(got_ref, out_ref):
    own = [got_ref[quarter_owners(q, R1_ROWS, OWN), :] for q in range(4)]
    total = jnp.concatenate([part[:, : 2 * S] for part in own], axis=1)
    ends = got_ref[pl.ds(OWN, D, stride=R1_ROWS), :][:, 2 * S : 2 * S + ENDS]
    for k in range(ENDS):
        part = got_ref[pl.ds(k, D, stride=R1_ROWS), :]
        total = total + select(end_matches(ends, k).astype(F32).T, part)
    for k in range(ENDS):
        out_ref[pl.ds(k, D, stride=G2_ROWS), :] = select(end_matches(ends, k), total)
    for q in range(4):
        own = [total[:, 2 * S * q : 2 * S * (q + 1)], jnp.zeros((NB, D - 2 * S), F32)]
        out_ref[quarter_owners(q, G2_ROWS, ENDS), :] = jnp.concatenate(own, axis=1)


def norm_kernel(mine_ref, other_ref, out_ref, norm_ref):
    norm_ref[...] = jnp.zeros((3 * S, 3 * S), F32)
    for ref in (mine_ref, other_ref):

        @pl.loop(0, N, step=8)
        def _(chip):
            wide = jnp.concatenate([ref[chip + i] for i in range(8)], axis=1)
            high, rest = split(wide)
            low = (wide - high.astype(F32) - rest.astype(F32)).astype(BF16)
            parts = jnp.concatenate([high, rest, low], axis=0)
            norm_ref[...] += lax.dot_general(parts, parts, NT, preferred_element_type=F32)

    norm = norm_ref[...]
    norm = norm[:S] + norm[S : 2 * S] + norm[2 * S :]
    norm = norm[:, :S] + norm[:, S : 2 * S] + norm[:, 2 * S :]
    unit = (iota((S, D), 0) == iota((S, D), 1) % S).astype(F32)
    out_ref[0] = widen(norm)
    out_ref[1] = gauss_solve(out_ref[0], unit)


def alpha_kernel(got_ref, norm_ref, right_ref, out_ref, begun_ref):
    row, rest = [
        jnp.sum(got_ref[pl.ds(at, D, stride=R1_ROWS), :], axis=0, keepdims=True)
        for at in (ENDS, OWN)
    ]
    rest = jnp.concatenate([rest[:, REST:], jnp.zeros((1, REST), F32)], axis=1)
    from_symmetric(row, rest, out_ref.at[0])
    out_ref[1] = gauss_solve(out_ref[0], norm_ref[0])
    begun_ref[...] = mixed(out_ref[1], right_ref[...])


def second_kernel(
    list_ref, mine_ref, other_ref, right_ref, ridge_ref, got_ref, small_ref, high_hbm, low_hbm,
    out_ref, keep_ref, high_ref, low_ref, gram_ref, sems,
):
    fetch = fetch_parts(high_hbm, low_hbm, high_ref, low_ref, sems)
    alpha_t = small_t(small_ref[1])[:, :S]

    def field(k):
        turned = got_ref[pl.ds(k, D, stride=G2_ROWS), :].T
        image = jnp.concatenate([turned[j * S : (j + 1) * S] for j in range(J)], axis=1)
        return block_of(mine_ref, other_ref, list_ref[k % 2, k // 2]) - exact(alpha_t, image)

    core = lax.axis_index("core")
    out_ref[...] = jnp.zeros(out_ref.shape, F32)

    def put(k, value):
        block = list_ref[k % 2, k // 2]
        for q in range(4):
            chip, side = 2 * block + q // 2, (q % 2 + core) % 2
            for j in range(2):
                rows = pl.ds(chip * SLOT + j * S, S)
                lanes = slice((2 * q + j) * D, (2 * q + j + 1) * D)
                out_ref[side, rows, :] = out_ref[side, rows, :] + value[:, lanes]

    right = right_ref[...]
    ridge = jnp.concatenate([ridge_ref[0:1], ridge_ref[1:2]], axis=1)
    turned = got_ref[pl.ds(ENDS, D, stride=G2_ROWS), :].T
    image = jnp.concatenate([turned[:S], turned[S : 2 * S]], axis=1)
    residual = right - exact(alpha_t, image)
    keep_ref[0] = residual
    keep_ref[1] = image
    gram_ref[0] = gram(residual, residual)
    gram_ref[1] = gram(residual, ridge * residual)
    gram_ref[1] += multiply(fetch, high_ref, low_ref, field, put)
    flat = jnp.concatenate([flat_rows(widen(gram_ref[i])) for i in range(2)], axis=0)
    for side in range(2):
        for chip in range(N):
            out_ref[side, chip * SLOT + GRAMS : (chip + 1) * SLOT, :] = flat


def last_kernel(
    got_ref, right_ref, ridge_ref, keep_ref, norm_ref, small_ref, begun_ref,
    solution_ref, residual_ref, gram_ref,
):
    total = got_ref[: 2 * SLOT]
    for chip in range(2, N, 2):
        total = total + got_ref[chip * SLOT : (chip + 2) * SLOT]
    total = total[:SLOT] + total[SLOT:]
    right = right_ref[...]
    residual, image = keep_ref[0], keep_ref[1]
    ridge = jnp.concatenate([ridge_ref[0:1], ridge_ref[1:2]], axis=1)
    second = jnp.concatenate([total[:S], total[S : 2 * S]], axis=1) + ridge * residual
    for i in range(2):
        gram_ref[i] = from_rows(total[GRAMS + 2 * i : GRAMS + 2 * i + 2])
    gram_ref[2] = small_mul(norm_ref[1], gram_ref[0])
    beta = gram_ref[2]
    gram_ref[3] = small_mul(small_t(beta), small_mul(small_ref[0], beta))
    last = gauss_solve(gram_ref[1] - gram_ref[3], gram_ref[0])
    direction = residual + mixed(beta, right)
    image_next = second + mixed(beta, image)
    solution_ref[...] = begun_ref[...] + mixed(last, direction)
    residual_ref[...] = residual - mixed(last, image_next)


HERE = pl.BlockSpec(memory_space=pltpu.VMEM)
SCALARS = pl.BlockSpec(memory_space=pltpu.SMEM)
THERE = pl.BlockSpec(memory_space=pltpu.HBM)
STAGED = [
    pltpu.VMEM((4, B, B), BF16),
    pltpu.VMEM((4, B, B), BF16),
]


def call(kernel, name, shapes, specs, args, scratch=(), limit=32):
    return pl.pallas_call(
        kernel,
        out_shape=[jax.ShapeDtypeStruct(shape, F32) for shape in shapes],
        in_specs=specs,
        out_specs=[HERE] * len(shapes),
        scratch_shapes=scratch,
        compiler_params=pltpu.CompilerParams(vmem_limit_bytes=limit << 20),
        name=name,
    )(*args)


def exchange_rows(x, rows):
    return lax.all_to_all(x.reshape(D, 1, rows * D), OWNERS, 0, 0).reshape(D * rows, D)


def swap(x):
    return lax.ppermute(x, "core", [(0, 1), (1, 0)])


def local(right, ridge, tiles, tile_list):
    ridge = ridge.reshape(2, D)
    tile_list = tile_list.T
    packed = jnp.broadcast_to(right, (N, S, 2 * D))
    later_list, packed = lax.optimization_barrier((tile_list, packed))
    staged = stage(tiles, later_list)
    mine = lax.all_to_all(packed, CHIPS, 0, 0)
    mine, *staged = lax.optimization_barrier((mine, *staged))
    other = swap(mine)
    sems = pltpu.SemaphoreType.DMA((2, len(PARTS)))
    (sent,) = call(
        first_kernel,
        "first",
        [(D * R1_ROWS, D)],
        [SCALARS] + [HERE] * 4 + [THERE] * 2,
        (tile_list, mine, other, right, ridge, *staged),
        [*STAGED, pltpu.VMEM((S, S), F32), pltpu.VMEM((D, D), F32), sems],
        48,
    )
    got = exchange_rows(sent, R1_ROWS)
    (sent,) = call(
        owner_kernel,
        "owner",
        [(D * G2_ROWS, D)],
        [HERE],
        (got,),
    )
    later_mine, sent = lax.optimization_barrier((mine, sent))
    (norm,) = call(
        norm_kernel,
        "norm",
        [(2, S, D)],
        [HERE] * 2,
        (later_mine, other),
        [pltpu.VMEM((3 * S, 3 * S), F32)],
    )
    small, begun = call(
        alpha_kernel, "alpha", [(2, S, D), (S, 2 * D)], [HERE] * 3, (got, norm, right)
    )
    got = exchange_rows(sent, G2_ROWS)
    sent, keep = call(
        second_kernel,
        "second",
        [(2, N * SLOT, D), (2, S, 2 * D)],
        [SCALARS] + [HERE] * 6 + [THERE] * 2,
        (tile_list, mine, other, right, ridge, got, small, *staged),
        [*STAGED, pltpu.VMEM((2, S, S), F32), sems],
        48,
    )
    sent = (sent[0] + swap(sent[1])).reshape(N, 1, SLOT * D)
    got = lax.all_to_all(sent, CHIPS, 0, 0).reshape(N * SLOT, D)
    return tuple(
        call(
            last_kernel,
            "last",
            [(S, 2 * D)] * 2,
            [HERE] * 7,
            (got, right, ridge, keep, norm, small, begun),
            [pltpu.VMEM((4, S, D), F32)],
        )
    )


def solution(mesh):
    mesh = jax.sharding.Mesh(mesh.devices.reshape(4, 16, 2), ALL)
    return jax.shard_map(
        local,
        mesh=mesh,
        in_specs=(P(None, ALL), P(ALL), P(ALL, None, None), P(ALL, None)),
        out_specs=(P(None, ALL), P(None, ALL)),
        check_vma=False,
    )
```

```python
import functools

import jax
import jax.numpy as jnp
from jax import lax
from jax.experimental import pallas as pl
from jax.experimental.pallas import tpu as pltpu
from jax.sharding import PartitionSpec as P

CHIPS = ("grp", "ring")
ALL = ("grp", "ring", "core")
OWNERS = ("core", "grp", "ring")
S = 16
B = 1024
NB = 32
D = 128
N = 64
J = 8
ENDS = 8
REST = 64
OWN = 9
SLOT = 36
GRAMS = 32
R1_ROWS = 10
G2_ROWS = 9
F32 = jnp.float32
BF16 = jnp.bfloat16
PIECE = 256
PIECES = B // PIECE
PARTS = [(0, 0, 256), (0, 256, 256), (0, 512, 512), (1, 0, B), (2, 0, B), (3, 0, B)]
NT = (((1,), (1,)), ((), ()))
NN = (((1,), (0,)), ((), ()))


def iota(shape, dim):
    return lax.broadcasted_iota(jnp.int32, shape, dim)


def exact(left, right):
    return jnp.dot(left, right, precision=lax.Precision.HIGHEST, preferred_element_type=F32)


def same_column():
    return (iota((D, D), 0) % S == iota((D, D), 1) % S).astype(F32)


def spread_sum(x):
    return exact(x, same_column())


def own_lanes():
    return iota((S, D), 1) // S == iota((S, D), 0) % 8


def flat_rows(g):
    kept = jnp.where(own_lanes(), g, 0.0)
    return jnp.concatenate(
        [jnp.sum(kept[:8], axis=0, keepdims=True), jnp.sum(kept[8:], axis=0, keepdims=True)], axis=0
    )


def from_rows(rows):
    top = jnp.broadcast_to(rows[0:1], (8, D))
    low = jnp.broadcast_to(rows[1:2], (8, D))
    return spread_sum(jnp.where(own_lanes(), jnp.concatenate([top, low], axis=0), 0.0))


def diagonals():
    lane = iota((S, D), 1)
    return iota((S, D), 0) == (lane % S + lane // S) % S


def opposite():
    return (iota((S, D), 0) == iota((S, D), 1) + S // 2) & (iota((S, D), 1) < S // 2)


def pack_symmetric(g):
    return [
        jnp.sum(jnp.where(keep, g, 0.0), axis=0, keepdims=True) for keep in (diagonals(), opposite())
    ]


def from_symmetric(row, rest, ref):
    lower = jnp.where(diagonals(), jnp.broadcast_to(row, (S, D)), 0.0)
    ref[...] = spread_sum(lower + jnp.where(opposite(), jnp.broadcast_to(rest, (S, D)), 0.0))
    middle = iota((S, D), 0) == iota((S, D), 1) % S
    ref[...] = ref[...] + jnp.where(middle, 0.0, small_t(ref[...]))


def stack8(g):
    return jnp.concatenate([g] * 8, axis=0)


def small_mul(left, right):
    return exact(jnp.where(iota((S, D), 1) < S, left, 0.0), stack8(right))


def small_t(g):
    return stack8(g).T[:S]


def gram(left, right):
    return lax.dot_general(
        left, right, NT, precision=lax.Precision.HIGHEST, preferred_element_type=F32
    )


def widen(g):
    return jnp.concatenate([g] * 8, axis=1)


def mixed(coeffs, rows):
    return exact(small_t(coeffs)[:, :S], rows)


def gauss_solve(matrix, rhs):
    lane = iota((S, D), 1)
    row = iota((S, D), 0)
    work = jnp.where(lane < S, matrix, rhs)
    for pivot in range(S):
        row_new = work[pivot : pivot + 1] * (1.0 / work[pivot : pivot + 1, pivot : pivot + 1])
        factor = jnp.where(row == pivot, 0.0, work[:, pivot : pivot + 1])
        work = jnp.where(row == pivot, row_new, work - factor * row_new)
    return spread_sum(jnp.where((lane >= S) & (lane < 2 * S), work, 0.0))


def split(x):
    high = x.astype(BF16)
    return high, (x - high.astype(F32)).astype(BF16)


def stage_kernel(list_ref, tiles_ref, high_ref, low_ref, held, high, low, in_sems, out_sems):
    def fetch(i):
        rows = pl.ds(i % PIECES * PIECE, PIECE)
        return pltpu.make_async_copy(tiles_ref.at[i // PIECES, rows], held.at[i], in_sems.at[i])

    def flush(i):
        rows = pl.ds(i % PIECES * PIECE, PIECE)
        return [
            pltpu.make_async_copy(here.at[i], there.at[i // PIECES, rows], out_sems.at[which, i])
            for which, (here, there) in enumerate(((high, high_ref), (low, low_ref)))
        ]

    for i in range(4 * PIECES):
        fetch(i).start()
    for i in range(4 * PIECES):
        fetch(i).wait()
        tile, first = i // PIECES, i % PIECES * PIECE
        high[i], low[i] = split(held[i])

        @pl.when(list_ref[0, tile] == list_ref[1, tile])
        def _():
            row, col = iota((PIECE, B), 0) + first, iota((PIECE, B), 1)
            kept = jnp.where(row > col, held[i], jnp.where(row == col, 0.5 * held[i], 0.0))
            high[i], low[i] = split(kept)

        for copy in flush(i):
            copy.start()
    for i in range(4 * PIECES):
        for copy in flush(i):
            copy.wait()


def stage(tiles, tile_list):
    anywhere = pl.BlockSpec(memory_space=pltpu.HBM)
    return pl.pallas_call(
        stage_kernel,
        out_shape=[pltpu.HBM((4, B, B), BF16)] * 2,
        in_specs=[pl.BlockSpec(memory_space=pltpu.SMEM), anywhere],
        out_specs=[anywhere] * 2,
        scratch_shapes=[
            pltpu.VMEM((4 * PIECES, PIECE, B), F32),
            pltpu.VMEM((4 * PIECES, PIECE, B), BF16),
            pltpu.VMEM((4 * PIECES, PIECE, B), BF16),
            pltpu.SemaphoreType.DMA((4 * PIECES,)),
            pltpu.SemaphoreType.DMA((2, 4 * PIECES)),
        ],
        compiler_params=pltpu.CompilerParams(vmem_limit_bytes=40 << 20),
        name="stage",
    )(tile_list, tiles)


def by_core(mine, other):
    first = lax.axis_index("core") == 0
    return jnp.where(first, mine, other), jnp.where(first, other, mine)


def block_of(mine_ref, other_ref, block):
    field = []
    for half in range(2):
        chip = 2 * block + half
        for piece in by_core(mine_ref[chip], other_ref[chip]):
            field += [piece[:, :D], piece[:, D:]]
    return jnp.concatenate(field, axis=1)


def fetch_parts(high_hbm, low_hbm, high_ref, low_ref, sems):
    def fetch(i):
        tile, first, rows = PARTS[i]
        part = (tile, pl.ds(first, rows))
        return [
            pltpu.make_async_copy(there.at[part], here.at[part], sems.at[which, i])
            for which, (there, here) in enumerate(((high_hbm, high_ref), (low_hbm, low_ref)))
        ]

    for i in range(1, len(PARTS)):
        for copy in fetch(i):
            copy.start()
    return fetch


def head_kernel(high_hbm, low_hbm, high_ref, low_ref, sems):
    part = (0, pl.ds(0, PARTS[0][2]))
    copies = [
        pltpu.make_async_copy(there.at[part], here, sems.at[which])
        for which, (there, here) in enumerate(((high_hbm, high_ref), (low_hbm, low_ref)))
    ]
    for copy in copies:
        copy.start()
    for copy in copies:
        copy.wait()


def head(staged):
    return pl.pallas_call(
        head_kernel,
        out_shape=[pltpu.VMEM((PARTS[0][2], B), BF16)] * 2,
        in_specs=[pl.BlockSpec(memory_space=pltpu.HBM)] * 2,
        out_specs=[pl.BlockSpec(memory_space=pltpu.VMEM)] * 2,
        scratch_shapes=[pltpu.SemaphoreType.DMA((2,))],
        name="head",
    )(*staged)


def multiply(fetch, high_ref, low_ref, heads, field, put):
    def product(vec, high, low, dims):
        vec_high, vec_low = split(vec)
        both = jnp.concatenate([vec_high, vec_low], axis=0)
        main = lax.dot_general(both, high[...], dims, preferred_element_type=F32)
        rest = lax.dot_general(vec_high, low[...], dims, preferred_element_type=F32)
        return main[:S] + (main[S:] + rest)

    half = jnp.zeros((S, S), F32)
    for tile in range(4):
        from_row, from_col = field(2 * tile), field(2 * tile + 1)
        into_row, into_col = [], []
        for i, (owner, first, rows) in enumerate(PARTS):
            if owner != tile:
                continue
            if i > 0:
                for copy in fetch(i):
                    copy.wait()
            at = slice(first, first + rows)
            parts = (high_ref.at[tile, at], low_ref.at[tile, at]) if i > 0 else heads
            into_row.append(product(from_col, *parts, NT))
            into_col.append(product(from_row[:, at], *parts, NN))
        into_row = jnp.concatenate(into_row, axis=1)
        put(2 * tile, into_row)
        put(2 * tile + 1, sum(into_col[1:], into_col[0]))
        half = half + gram(from_row, into_row)
    return half + half.T


def first_kernel(
    list_ref, mine_ref, other_ref, right_ref, ridge_ref, head_high, head_low, high_hbm, low_hbm,
    out_ref, high_ref, low_ref, gram_ref, own_ref, sems,
):
    fetch = fetch_parts(high_hbm, low_hbm, high_ref, low_ref, sems)

    def field(k):
        return block_of(mine_ref, other_ref, list_ref[k % 2, k // 2])

    def put(k, value):
        tall = jnp.concatenate([value[:, j * D : (j + 1) * D] for j in range(J)], axis=0)
        out_ref[pl.ds(k, D, stride=R1_ROWS), :] = tall.T

    right = right_ref[...]
    scaled = jnp.concatenate([ridge_ref[0:1], ridge_ref[1:2]], axis=1) * right
    gram_ref[...] = gram(right, scaled)
    slot = iota((ENDS, D), 0)
    ends = jnp.zeros((ENDS, D), F32)
    for k in range(ENDS):
        ends = jnp.where(slot == k, list_ref[k % 2, k // 2].astype(F32), ends)
    own = [scaled[:, :D], scaled[:, D:], ends, jnp.zeros((D - 2 * S - ENDS, D), F32)]
    own_ref[...] = jnp.concatenate(own, axis=0).T
    curvature = multiply(fetch, high_ref, low_ref, (head_high, head_low), field, put)
    row, rest = pack_symmetric(widen(gram_ref[...] + curvature))
    out_ref[pl.ds(ENDS, D, stride=R1_ROWS), :] = jnp.broadcast_to(row, (D, D))
    rest = jnp.concatenate([jnp.zeros((1, REST), F32), rest[:, : D - REST]], axis=1)
    out_ref[pl.ds(OWN, D, stride=R1_ROWS), :] = own_ref[...] + rest


def end_matches(ends, k):
    return ends[:, k : k + 1] == iota((D, NB), 1).astype(F32)


def select(matches, values):
    high, rest = split(values)
    low = (values - high.astype(F32) - rest.astype(F32)).astype(BF16)
    parts = jnp.dot(
        matches.astype(F32).astype(BF16),
        jnp.concatenate([high, rest, low], axis=1),
        preferred_element_type=F32,
    )
    return parts[:, :D] + parts[:, D : 2 * D] + parts[:, 2 * D :]


def quarter_owners(q, rows, row):
    return pl.ds(rows * (q % 2 * N + q // 2) + row, NB, stride=2 * rows)


def owner_kernel(got_ref, out_ref):
    own = [got_ref[quarter_owners(q, R1_ROWS, OWN), :] for q in range(4)]
    total = jnp.concatenate([part[:, : 2 * S] for part in own], axis=1)
    ends = got_ref[pl.ds(OWN, D, stride=R1_ROWS), :][:, 2 * S : 2 * S + ENDS]
    for k in range(ENDS):
        part = got_ref[pl.ds(k, D, stride=R1_ROWS), :]
        total = total + select(end_matches(ends, k).astype(F32).T, part)
    for k in range(ENDS):
        out_ref[pl.ds(k, D, stride=G2_ROWS), :] = select(end_matches(ends, k), total)
    for q in range(4):
        own = [total[:, 2 * S * q : 2 * S * (q + 1)], jnp.zeros((NB, D - 2 * S), F32)]
        out_ref[quarter_owners(q, G2_ROWS, ENDS), :] = jnp.concatenate(own, axis=1)


def norm_kernel(mine_ref, other_ref, out_ref, norm_ref):
    norm_ref[...] = jnp.zeros((3 * S, 3 * S), F32)
    for ref in (mine_ref, other_ref):

        @pl.loop(0, N, step=8)
        def _(chip):
            wide = jnp.concatenate([ref[chip + i] for i in range(8)], axis=1)
            high, rest = split(wide)
            low = (wide - high.astype(F32) - rest.astype(F32)).astype(BF16)
            parts = jnp.concatenate([high, rest, low], axis=0)
            norm_ref[...] += lax.dot_general(parts, parts, NT, preferred_element_type=F32)

    norm = norm_ref[...]
    norm = norm[:S] + norm[S : 2 * S] + norm[2 * S :]
    norm = norm[:, :S] + norm[:, S : 2 * S] + norm[:, 2 * S :]
    unit = (iota((S, D), 0) == iota((S, D), 1) % S).astype(F32)
    out_ref[0] = widen(norm)
    out_ref[1] = gauss_solve(out_ref[0], unit)


def alpha_kernel(got_ref, norm_ref, right_ref, out_ref, begun_ref):
    row, rest = [
        jnp.sum(got_ref[pl.ds(at, D, stride=R1_ROWS), :], axis=0, keepdims=True)
        for at in (ENDS, OWN)
    ]
    rest = jnp.concatenate([rest[:, REST:], jnp.zeros((1, REST), F32)], axis=1)
    from_symmetric(row, rest, out_ref.at[0])
    out_ref[1] = gauss_solve(out_ref[0], norm_ref[0])
    begun_ref[...] = mixed(out_ref[1], right_ref[...])


def second_kernel(
    list_ref, mine_ref, other_ref, right_ref, ridge_ref, got_ref, small_ref, head_high, head_low,
    high_hbm, low_hbm, out_ref, keep_ref, high_ref, low_ref, gram_ref, sems,
):
    fetch = fetch_parts(high_hbm, low_hbm, high_ref, low_ref, sems)
    alpha_t = small_t(small_ref[1])[:, :S]

    def field(k):
        turned = got_ref[pl.ds(k, D, stride=G2_ROWS), :].T
        image = jnp.concatenate([turned[j * S : (j + 1) * S] for j in range(J)], axis=1)
        return block_of(mine_ref, other_ref, list_ref[k % 2, k // 2]) - exact(alpha_t, image)

    core = lax.axis_index("core")
    out_ref[...] = jnp.zeros(out_ref.shape, F32)

    def put(k, value):
        block = list_ref[k % 2, k // 2]
        for q in range(4):
            chip, side = 2 * block + q // 2, (q % 2 + core) % 2
            for j in range(2):
                rows = pl.ds(chip * SLOT + j * S, S)
                lanes = slice((2 * q + j) * D, (2 * q + j + 1) * D)
                out_ref[side, rows, :] = out_ref[side, rows, :] + value[:, lanes]

    right = right_ref[...]
    ridge = jnp.concatenate([ridge_ref[0:1], ridge_ref[1:2]], axis=1)
    turned = got_ref[pl.ds(ENDS, D, stride=G2_ROWS), :].T
    image = jnp.concatenate([turned[:S], turned[S : 2 * S]], axis=1)
    residual = right - exact(alpha_t, image)
    keep_ref[0] = residual
    keep_ref[1] = image
    gram_ref[0] = gram(residual, residual)
    gram_ref[1] = gram(residual, ridge * residual)
    gram_ref[1] += multiply(fetch, high_ref, low_ref, (head_high, head_low), field, put)
    flat = jnp.concatenate([flat_rows(widen(gram_ref[i])) for i in range(2)], axis=0)
    for side in range(2):
        for chip in range(N):
            out_ref[side, chip * SLOT + GRAMS : (chip + 1) * SLOT, :] = flat


def last_kernel(
    got_ref, right_ref, ridge_ref, keep_ref, norm_ref, small_ref, begun_ref,
    solution_ref, residual_ref, gram_ref,
):
    total = got_ref[: 2 * SLOT]
    for chip in range(2, N, 2):
        total = total + got_ref[chip * SLOT : (chip + 2) * SLOT]
    total = total[:SLOT] + total[SLOT:]
    right = right_ref[...]
    residual, image = keep_ref[0], keep_ref[1]
    ridge = jnp.concatenate([ridge_ref[0:1], ridge_ref[1:2]], axis=1)
    second = jnp.concatenate([total[:S], total[S : 2 * S]], axis=1) + ridge * residual
    for i in range(2):
        gram_ref[i] = from_rows(total[GRAMS + 2 * i : GRAMS + 2 * i + 2])
    gram_ref[2] = small_mul(norm_ref[1], gram_ref[0])
    beta = gram_ref[2]
    gram_ref[3] = small_mul(small_t(beta), small_mul(small_ref[0], beta))
    last = gauss_solve(gram_ref[1] - gram_ref[3], gram_ref[0])
    direction = residual + mixed(beta, right)
    image_next = second + mixed(beta, image)
    solution_ref[...] = begun_ref[...] + mixed(last, direction)
    residual_ref[...] = residual - mixed(last, image_next)


HERE = pl.BlockSpec(memory_space=pltpu.VMEM)
SCALARS = pl.BlockSpec(memory_space=pltpu.SMEM)
THERE = pl.BlockSpec(memory_space=pltpu.HBM)
STAGED = [
    pltpu.VMEM((4, B, B), BF16),
    pltpu.VMEM((4, B, B), BF16),
]


def call(kernel, name, shapes, specs, args, scratch=(), limit=32):
    return pl.pallas_call(
        kernel,
        out_shape=[jax.ShapeDtypeStruct(shape, F32) for shape in shapes],
        in_specs=specs,
        out_specs=[HERE] * len(shapes),
        scratch_shapes=scratch,
        compiler_params=pltpu.CompilerParams(vmem_limit_bytes=limit << 20),
        name=name,
    )(*args)


def exchange_rows(x, rows):
    return lax.all_to_all(x.reshape(D, 1, rows * D), OWNERS, 0, 0).reshape(D * rows, D)


def swap(x):
    return lax.ppermute(x, "core", [(0, 1), (1, 0)])


def local(right, ridge, tiles, tile_list):
    ridge = ridge.reshape(2, D)
    tile_list = tile_list.T
    packed = jnp.broadcast_to(right, (N, S, 2 * D))
    later_list, packed = lax.optimization_barrier((tile_list, packed))
    staged = stage(tiles, later_list)
    mine = lax.all_to_all(packed, CHIPS, 0, 0)
    mine, *staged = lax.optimization_barrier((mine, *staged))
    heads = head(staged)
    other = swap(mine)
    other, *heads = lax.optimization_barrier((other, *heads))
    sems = pltpu.SemaphoreType.DMA((2, len(PARTS)))
    (sent,) = call(
        first_kernel,
        "first",
        [(D * R1_ROWS, D)],
        [SCALARS] + [HERE] * 6 + [THERE] * 2,
        (tile_list, mine, other, right, ridge, *heads, *staged),
        [*STAGED, pltpu.VMEM((S, S), F32), pltpu.VMEM((D, D), F32), sems],
        48,
    )
    got = exchange_rows(sent, R1_ROWS)
    (sent,) = call(
        owner_kernel,
        "owner",
        [(D * G2_ROWS, D)],
        [HERE],
        (got,),
    )
    later_mine, sent = lax.optimization_barrier((mine, sent))
    (norm,) = call(
        norm_kernel,
        "norm",
        [(2, S, D)],
        [HERE] * 2,
        (later_mine, other),
        [pltpu.VMEM((3 * S, 3 * S), F32)],
    )
    small, begun = call(
        alpha_kernel, "alpha", [(2, S, D), (S, 2 * D)], [HERE] * 3, (got, norm, right)
    )
    later_high, small = lax.optimization_barrier((staged[0], small))
    heads = head((later_high, staged[1]))
    got = exchange_rows(sent, G2_ROWS)
    got, *heads = lax.optimization_barrier((got, *heads))
    sent, keep = call(
        second_kernel,
        "second",
        [(2, N * SLOT, D), (2, S, 2 * D)],
        [SCALARS] + [HERE] * 8 + [THERE] * 2,
        (tile_list, mine, other, right, ridge, got, small, *heads, *staged),
        [*STAGED, pltpu.VMEM((2, S, S), F32), sems],
        48,
    )
    sent = (sent[0] + swap(sent[1])).reshape(N, 1, SLOT * D)
    got = lax.all_to_all(sent, CHIPS, 0, 0).reshape(N * SLOT, D)
    return tuple(
        call(
            last_kernel,
            "last",
            [(S, 2 * D)] * 2,
            [HERE] * 7,
            (got, right, ridge, keep, norm, small, begun),
            [pltpu.VMEM((4, S, D), F32)],
        )
    )


def solution(mesh):
    mesh = jax.sharding.Mesh(mesh.devices.reshape(4, 16, 2), ALL)
    return jax.shard_map(
        local,
        mesh=mesh,
        in_specs=(P(None, ALL), P(ALL), P(ALL, None, None), P(ALL, None)),
        out_specs=(P(None, ALL), P(None, ALL)),
        check_vma=False,
    )
```

```python
import functools

import jax
import jax.numpy as jnp
from jax import lax
from jax.experimental import pallas as pl
from jax.experimental.pallas import tpu as pltpu
from jax.sharding import PartitionSpec as P

CHIPS = ("grp", "ring")
ALL = ("grp", "ring", "core")
OWNERS = ("core", "grp", "ring")
S = 16
B = 1024
NB = 32
D = 128
N = 64
J = 8
ENDS = 8
REST = 64
OWN = 9
SLOT = 36
GRAMS = 32
R1_ROWS = 10
G2_ROWS = 9
F32 = jnp.float32
BF16 = jnp.bfloat16
PIECE = 256
PIECES = B // PIECE
PARTS = [(0, 0, 256), (0, 256, 256), (0, 512, 512), (1, 0, B), (2, 0, B), (3, 0, B)]
NT = (((1,), (1,)), ((), ()))
NN = (((1,), (0,)), ((), ()))


def iota(shape, dim):
    return lax.broadcasted_iota(jnp.int32, shape, dim)


def exact(left, right):
    return jnp.dot(left, right, precision=lax.Precision.HIGHEST, preferred_element_type=F32)


def same_column():
    return (iota((D, D), 0) % S == iota((D, D), 1) % S).astype(F32)


def spread_sum(x):
    return exact(x, same_column())


def own_lanes():
    return iota((S, D), 1) // S == iota((S, D), 0) % 8


def flat_rows(g):
    kept = jnp.where(own_lanes(), g, 0.0)
    return jnp.concatenate(
        [jnp.sum(kept[:8], axis=0, keepdims=True), jnp.sum(kept[8:], axis=0, keepdims=True)], axis=0
    )


def from_rows(rows):
    top = jnp.broadcast_to(rows[0:1], (8, D))
    low = jnp.broadcast_to(rows[1:2], (8, D))
    return spread_sum(jnp.where(own_lanes(), jnp.concatenate([top, low], axis=0), 0.0))


def diagonals():
    lane = iota((S, D), 1)
    return iota((S, D), 0) == (lane % S + lane // S) % S


def opposite():
    return (iota((S, D), 0) == iota((S, D), 1) + S // 2) & (iota((S, D), 1) < S // 2)


def pack_symmetric(g):
    return [
        jnp.sum(jnp.where(keep, g, 0.0), axis=0, keepdims=True) for keep in (diagonals(), opposite())
    ]


def from_symmetric(row, rest, ref):
    lower = jnp.where(diagonals(), jnp.broadcast_to(row, (S, D)), 0.0)
    ref[...] = spread_sum(lower + jnp.where(opposite(), jnp.broadcast_to(rest, (S, D)), 0.0))
    middle = iota((S, D), 0) == iota((S, D), 1) % S
    ref[...] = ref[...] + jnp.where(middle, 0.0, small_t(ref[...]))


def stack8(g):
    return jnp.concatenate([g] * 8, axis=0)


def small_mul(left, right):
    return exact(jnp.where(iota((S, D), 1) < S, left, 0.0), stack8(right))


def small_t(g):
    return stack8(g).T[:S]


def gram(left, right):
    return lax.dot_general(
        left, right, NT, precision=lax.Precision.HIGHEST, preferred_element_type=F32
    )


def widen(g):
    return jnp.concatenate([g] * 8, axis=1)


def mixed(coeffs, rows):
    return exact(small_t(coeffs)[:, :S], rows)


def gauss_solve(matrix, rhs):
    lane = iota((S, D), 1)
    row = iota((S, D), 0)
    work = jnp.where(lane < S, matrix, rhs)
    for pivot in range(S):
        row_new = work[pivot : pivot + 1] * (1.0 / work[pivot : pivot + 1, pivot : pivot + 1])
        factor = jnp.where(row == pivot, 0.0, work[:, pivot : pivot + 1])
        work = jnp.where(row == pivot, row_new, work - factor * row_new)
    return spread_sum(jnp.where((lane >= S) & (lane < 2 * S), work, 0.0))


def split(x):
    high = x.astype(BF16)
    return high, (x - high.astype(F32)).astype(BF16)


def stage_kernel(list_ref, tiles_ref, high_ref, low_ref, held, high, low, in_sems, out_sems):
    def fetch(i):
        rows = pl.ds(i % PIECES * PIECE, PIECE)
        return pltpu.make_async_copy(tiles_ref.at[i // PIECES, rows], held.at[i], in_sems.at[i])

    def flush(i):
        rows = pl.ds(i % PIECES * PIECE, PIECE)
        return [
            pltpu.make_async_copy(here.at[i], there.at[i // PIECES, rows], out_sems.at[which, i])
            for which, (here, there) in enumerate(((high, high_ref), (low, low_ref)))
        ]

    for i in range(4 * PIECES):
        fetch(i).start()
    for i in range(4 * PIECES):
        fetch(i).wait()
        tile, first = i // PIECES, i % PIECES * PIECE
        high[i], low[i] = split(held[i])

        @pl.when(list_ref[0, tile] == list_ref[1, tile])
        def _():
            row, col = iota((PIECE, B), 0) + first, iota((PIECE, B), 1)
            kept = jnp.where(row > col, held[i], jnp.where(row == col, 0.5 * held[i], 0.0))
            high[i], low[i] = split(kept)

        for copy in flush(i):
            copy.start()
    for i in range(4 * PIECES):
        for copy in flush(i):
            copy.wait()


def stage(tiles, tile_list):
    anywhere = pl.BlockSpec(memory_space=pltpu.HBM)
    return pl.pallas_call(
        stage_kernel,
        out_shape=[pltpu.HBM((4, B, B), BF16)] * 2,
        in_specs=[pl.BlockSpec(memory_space=pltpu.SMEM), anywhere],
        out_specs=[anywhere] * 2,
        scratch_shapes=[
            pltpu.VMEM((4 * PIECES, PIECE, B), F32),
            pltpu.VMEM((4 * PIECES, PIECE, B), BF16),
            pltpu.VMEM((4 * PIECES, PIECE, B), BF16),
            pltpu.SemaphoreType.DMA((4 * PIECES,)),
            pltpu.SemaphoreType.DMA((2, 4 * PIECES)),
        ],
        compiler_params=pltpu.CompilerParams(vmem_limit_bytes=40 << 20),
        name="stage",
    )(tile_list, tiles)


def by_core(mine, other):
    first = lax.axis_index("core") == 0
    return jnp.where(first, mine, other), jnp.where(first, other, mine)


def block_of(mine_ref, other_ref, block):
    field = []
    for half in range(2):
        chip = 2 * block + half
        for piece in by_core(mine_ref[chip], other_ref[chip]):
            field += [piece[:, :D], piece[:, D:]]
    return jnp.concatenate(field, axis=1)


def fetch_parts(high_hbm, low_hbm, high_ref, low_ref, sems):
    def fetch(i):
        tile, first, rows = PARTS[i]
        part = (tile, pl.ds(first, rows))
        return [
            pltpu.make_async_copy(there.at[part], here.at[part], sems.at[which, i])
            for which, (there, here) in enumerate(((high_hbm, high_ref), (low_hbm, low_ref)))
        ]

    for i in range(len(PARTS)):
        for copy in fetch(i):
            copy.start()
    return fetch


def multiply(fetch, high_ref, low_ref, field, put):
    def product(vec, tile, part, dims):
        vec_high, vec_low = split(vec)
        both = jnp.concatenate([vec_high, vec_low], axis=0)
        main = lax.dot_general(both, high_ref[tile, part], dims, preferred_element_type=F32)
        rest = lax.dot_general(vec_high, low_ref[tile, part], dims, preferred_element_type=F32)
        return main[:S] + (main[S:] + rest)

    half = jnp.zeros((S, S), F32)
    for tile in range(4):
        from_row, from_col = field(2 * tile), field(2 * tile + 1)
        into_row, into_col = [], []
        for i, (owner, first, rows) in enumerate(PARTS):
            if owner != tile:
                continue
            for copy in fetch(i):
                copy.wait()
            at = slice(first, first + rows)
            into_row.append(product(from_col, tile, at, NT))
            into_col.append(product(from_row[:, at], tile, at, NN))
        into_row = jnp.concatenate(into_row, axis=1)
        put(2 * tile, into_row)
        put(2 * tile + 1, sum(into_col[1:], into_col[0]))
        half = half + gram(from_row, into_row)
    return half + half.T


def first_kernel(
    list_ref, mine_ref, other_ref, right_ref, ridge_ref, high_hbm, low_hbm, out_ref,
    high_ref, low_ref, gram_ref, own_ref, sems,
):
    fetch = fetch_parts(high_hbm, low_hbm, high_ref, low_ref, sems)

    def field(k):
        return block_of(mine_ref, other_ref, list_ref[k % 2, k // 2])

    def put(k, value):
        tall = jnp.concatenate([value[:, j * D : (j + 1) * D] for j in range(J)], axis=0)
        out_ref[pl.ds(k, D, stride=R1_ROWS), :] = tall.T

    right = right_ref[...]
    scaled = jnp.concatenate([ridge_ref[0:1], ridge_ref[1:2]], axis=1) * right
    gram_ref[...] = gram(right, scaled)
    slot = iota((ENDS, D), 0)
    ends = jnp.zeros((ENDS, D), F32)
    for k in range(ENDS):
        ends = jnp.where(slot == k, list_ref[k % 2, k // 2].astype(F32), ends)
    own = [scaled[:, :D], scaled[:, D:], ends, jnp.zeros((D - 2 * S - ENDS, D), F32)]
    own_ref[...] = jnp.concatenate(own, axis=0).T
    curvature = multiply(fetch, high_ref, low_ref, field, put)
    row, rest = pack_symmetric(widen(gram_ref[...] + curvature))
    out_ref[pl.ds(ENDS, D, stride=R1_ROWS), :] = jnp.broadcast_to(row, (D, D))
    rest = jnp.concatenate([jnp.zeros((1, REST), F32), rest[:, : D - REST]], axis=1)
    out_ref[pl.ds(OWN, D, stride=R1_ROWS), :] = own_ref[...] + rest


def end_matches(ends, k):
    return ends[:, k : k + 1] == iota((D, NB), 1).astype(F32)


def select(matches, values):
    high, rest = split(values)
    low = (values - high.astype(F32) - rest.astype(F32)).astype(BF16)
    parts = jnp.dot(
        matches.astype(F32).astype(BF16),
        jnp.concatenate([high, rest, low], axis=1),
        preferred_element_type=F32,
    )
    return parts[:, :D] + parts[:, D : 2 * D] + parts[:, 2 * D :]


def quarter_owners(q, rows, row):
    return pl.ds(rows * (q % 2 * N + q // 2) + row, NB, stride=2 * rows)


def owner_kernel(got_ref, out_ref):
    own = [got_ref[quarter_owners(q, R1_ROWS, OWN), :] for q in range(4)]
    total = jnp.concatenate([part[:, : 2 * S] for part in own], axis=1)
    ends = got_ref[pl.ds(OWN, D, stride=R1_ROWS), :][:, 2 * S : 2 * S + ENDS]
    for k in range(ENDS):
        part = got_ref[pl.ds(k, D, stride=R1_ROWS), :]
        total = total + select(end_matches(ends, k).astype(F32).T, part)
    for k in range(ENDS):
        out_ref[pl.ds(k, D, stride=G2_ROWS), :] = select(end_matches(ends, k), total)
    for q in range(4):
        own = [total[:, 2 * S * q : 2 * S * (q + 1)], jnp.zeros((NB, D - 2 * S), F32)]
        out_ref[quarter_owners(q, G2_ROWS, ENDS), :] = jnp.concatenate(own, axis=1)


def norm_kernel(mine_ref, other_ref, out_ref, norm_ref):
    norm_ref[...] = jnp.zeros((3 * S, 3 * S), F32)
    for ref in (mine_ref, other_ref):

        @pl.loop(0, N, step=8)
        def _(chip):
            wide = jnp.concatenate([ref[chip + i] for i in range(8)], axis=1)
            high, rest = split(wide)
            low = (wide - high.astype(F32) - rest.astype(F32)).astype(BF16)
            parts = jnp.concatenate([high, rest, low], axis=0)
            norm_ref[...] += lax.dot_general(parts, parts, NT, preferred_element_type=F32)

    norm = norm_ref[...]
    norm = norm[:S] + norm[S : 2 * S] + norm[2 * S :]
    norm = norm[:, :S] + norm[:, S : 2 * S] + norm[:, 2 * S :]
    unit = (iota((S, D), 0) == iota((S, D), 1) % S).astype(F32)
    out_ref[0] = widen(norm)
    out_ref[1] = gauss_solve(out_ref[0], unit)


def alpha_kernel(got_ref, norm_ref, right_ref, out_ref, begun_ref):
    row, rest = [
        jnp.sum(got_ref[pl.ds(at, D, stride=R1_ROWS), :], axis=0, keepdims=True)
        for at in (ENDS, OWN)
    ]
    rest = jnp.concatenate([rest[:, REST:], jnp.zeros((1, REST), F32)], axis=1)
    from_symmetric(row, rest, out_ref.at[0])
    out_ref[1] = gauss_solve(out_ref[0], norm_ref[0])
    begun_ref[...] = mixed(out_ref[1], right_ref[...])


def second_kernel(
    list_ref, mine_ref, other_ref, right_ref, ridge_ref, got_ref, small_ref, high_hbm, low_hbm,
    out_ref, keep_ref, high_ref, low_ref, gram_ref, sems,
):
    fetch = fetch_parts(high_hbm, low_hbm, high_ref, low_ref, sems)
    alpha_t = small_t(small_ref[1])[:, :S]

    def field(k):
        turned = got_ref[pl.ds(k, D, stride=G2_ROWS), :].T
        image = jnp.concatenate([turned[j * S : (j + 1) * S] for j in range(J)], axis=1)
        return block_of(mine_ref, other_ref, list_ref[k % 2, k // 2]) - exact(alpha_t, image)

    core = lax.axis_index("core")
    out_ref[...] = jnp.zeros(out_ref.shape, F32)

    def put(k, value):
        block = list_ref[k % 2, k // 2]
        for q in range(4):
            chip, side = 2 * block + q // 2, (q % 2 + core) % 2
            for j in range(2):
                rows = pl.ds(chip * SLOT + j * S, S)
                lanes = slice((2 * q + j) * D, (2 * q + j + 1) * D)
                out_ref[side, rows, :] = out_ref[side, rows, :] + value[:, lanes]

    right = right_ref[...]
    ridge = jnp.concatenate([ridge_ref[0:1], ridge_ref[1:2]], axis=1)
    turned = got_ref[pl.ds(ENDS, D, stride=G2_ROWS), :].T
    image = jnp.concatenate([turned[:S], turned[S : 2 * S]], axis=1)
    residual = right - exact(alpha_t, image)
    keep_ref[0] = residual
    keep_ref[1] = image
    gram_ref[0] = gram(residual, residual)
    gram_ref[1] = gram(residual, ridge * residual)
    gram_ref[1] += multiply(fetch, high_ref, low_ref, field, put)
    flat = jnp.concatenate([flat_rows(widen(gram_ref[i])) for i in range(2)], axis=0)
    for side in range(2):
        for chip in range(N):
            out_ref[side, chip * SLOT + GRAMS : (chip + 1) * SLOT, :] = flat


def last_kernel(
    got_ref, right_ref, ridge_ref, keep_ref, norm_ref, small_ref, begun_ref,
    solution_ref, residual_ref, gram_ref,
):
    total = got_ref[: 2 * SLOT]
    for chip in range(2, N, 2):
        total = total + got_ref[chip * SLOT : (chip + 2) * SLOT]
    total = total[:SLOT] + total[SLOT:]
    right = right_ref[...]
    residual, image = keep_ref[0], keep_ref[1]
    ridge = jnp.concatenate([ridge_ref[0:1], ridge_ref[1:2]], axis=1)
    second = jnp.concatenate([total[:S], total[S : 2 * S]], axis=1) + ridge * residual
    for i in range(2):
        gram_ref[i] = from_rows(total[GRAMS + 2 * i : GRAMS + 2 * i + 2])
    gram_ref[2] = small_mul(norm_ref[1], gram_ref[0])
    beta = gram_ref[2]
    gram_ref[3] = small_mul(small_t(beta), small_mul(small_ref[0], beta))
    last = gauss_solve(gram_ref[1] - gram_ref[3], gram_ref[0])
    direction = residual + mixed(beta, right)
    image_next = second + mixed(beta, image)
    solution_ref[...] = begun_ref[...] + mixed(last, direction)
    residual_ref[...] = residual - mixed(last, image_next)


HERE = pl.BlockSpec(memory_space=pltpu.VMEM)
SCALARS = pl.BlockSpec(memory_space=pltpu.SMEM)
THERE = pl.BlockSpec(memory_space=pltpu.HBM)
STAGED = [
    pltpu.VMEM((4, B, B), BF16),
    pltpu.VMEM((4, B, B), BF16),
]


def call(kernel, name, shapes, specs, args, scratch=(), limit=32):
    return pl.pallas_call(
        kernel,
        out_shape=[jax.ShapeDtypeStruct(shape, F32) for shape in shapes],
        in_specs=specs,
        out_specs=[HERE] * len(shapes),
        scratch_shapes=scratch,
        compiler_params=pltpu.CompilerParams(vmem_limit_bytes=limit << 20),
        name=name,
    )(*args)


def exchange_rows(x, rows):
    return lax.all_to_all(x.reshape(D, 1, rows * D), OWNERS, 0, 0).reshape(D * rows, D)


def swap(x):
    return lax.ppermute(x, "core", [(0, 1), (1, 0)])


def local(right, ridge, tiles, tile_list):
    ridge = ridge.reshape(2, D)
    tile_list = tile_list.T
    packed = jnp.broadcast_to(right, (N, S, 2 * D))
    later_list, packed = lax.optimization_barrier((tile_list, packed))
    staged = stage(tiles, later_list)
    mine = lax.all_to_all(packed, CHIPS, 0, 0)
    mine, *staged = lax.optimization_barrier((mine, *staged))
    other = swap(mine)
    sems = pltpu.SemaphoreType.DMA((2, len(PARTS)))
    (sent,) = call(
        first_kernel,
        "first",
        [(D * R1_ROWS, D)],
        [SCALARS] + [HERE] * 4 + [THERE] * 2,
        (tile_list, mine, other, right, ridge, *staged),
        [*STAGED, pltpu.VMEM((S, S), F32), pltpu.VMEM((D, D), F32), sems],
        48,
    )
    got = exchange_rows(sent, R1_ROWS)
    (sent,) = call(
        owner_kernel,
        "owner",
        [(D * G2_ROWS, D)],
        [HERE],
        (got,),
    )
    later_mine, sent = lax.optimization_barrier((mine, sent))
    (norm,) = call(
        norm_kernel,
        "norm",
        [(2, S, D)],
        [HERE] * 2,
        (later_mine, other),
        [pltpu.VMEM((3 * S, 3 * S), F32)],
    )
    small, begun = call(
        alpha_kernel, "alpha", [(2, S, D), (S, 2 * D)], [HERE] * 3, (got, norm, right)
    )
    got = exchange_rows(sent, G2_ROWS)
    sent, keep = call(
        second_kernel,
        "second",
        [(2, N * SLOT, D), (2, S, 2 * D)],
        [SCALARS] + [HERE] * 6 + [THERE] * 2,
        (tile_list, mine, other, right, ridge, got, small, *staged),
        [*STAGED, pltpu.VMEM((2, S, S), F32), sems],
        48,
    )
    sent = (sent[0] + swap(sent[1])).reshape(N, 1, SLOT * D)
    got = lax.all_to_all(sent, CHIPS, 0, 0).reshape(N * SLOT, D)
    return tuple(
        call(
            last_kernel,
            "last",
            [(S, 2 * D)] * 2,
            [HERE] * 7,
            (got, right, ridge, keep, norm, small, begun),
            [pltpu.VMEM((4, S, D), F32)],
        )
    )


def solution(mesh):
    mesh = jax.sharding.Mesh(mesh.devices.reshape(4, 16, 2), ALL)
    return jax.shard_map(
        local,
        mesh=mesh,
        in_specs=(P(None, ALL), P(ALL), P(ALL, None, None), P(ALL, None)),
        out_specs=(P(None, ALL), P(None, ALL)),
        check_vma=False,
    )
```
